32 devices in a mesh: gx: 4 (over y, x), gz: 4 (over z), gy: 2 (over core).
Axes of the slice: x: 2, y: 2, z: 4, core: 2. Of those that a mesh axis runs over, the one named last changes fastest.
Arguments:
- blocks: bfloat16 [4, 4, 4, 96, 4096], P('gx', 'gz', 'gy'), may hold values from -6 to 6
- block_count: int32 [4, 4, 2], P('gx', 'gz', 'gy'), may hold values from 1 to 2, as said below
- neighbours: int32 [4, 4, 4, 26], P('gx', 'gz', 'gy'), may hold values from -1 to 15, as said below
- conv_weight: bfloat16 [48, 2592], replicated, may hold values from -0.125 to 0.125
- conv_bias: float32 [48], replicated, may hold values from -3 to 3
- head_weight: bfloat16 [48, 48], replicated, may hold values from -0.875 to 0.875
- head_bias: float32 [48], replicated, may hold values from -3 to 3
Outputs:
- features: bfloat16 [4, 4, 4, 48, 4096], P('gx', 'gz', 'gy')
The draws below stay inside these ranges and needn't reach their ends.
Inputs may be any that keep to these rules, and one draw needn't show every extreme that they name: Each device's foreground blocks fill its first block_count slots; some device fills all 2. `neighbours`: -1 means no foreground block at that offset. Otherwise the value is u + 2 c: used slot u of the device reached from this one by the offset's steps along the axes whose bits are set in c (bit 0 x, bit 1 y, bit 2 z); bits are set only on axes where the offset is nonzero, and c = 0 names this device. Unused slots hold -1 everywhere. Each device's blocks sit at distinct positions of its own region of 2 x 2 x 4 block positions, and the links follow that geometry. The most is reached in every draw.
All inputs are finite; a program needn't handle non-finite values.
Results may differ from the reference program's by a relative error of at most 0.0046.
Values may be sent and summed in bfloat16 or wider, within the bound.
A program may use at most 128 MiB of HBM per device.

```python
import jax
import jax.numpy as jnp
from jax import lax

CIN = 96
COUT = 48
EDGE = 16
VOX = 4096
SLOTS = 2
RX = 2
RY = 2
RZ = 4
N_GX = 4
N_GZ = 4
N_GY = 2


def permute_region(subkey):
    return jax.random.permutation(subkey, RX * RY * RZ)


def place_value(row, index, value):
    where_now = jnp.argmax((row == value).astype(jnp.int32)).astype(jnp.int32)
    current = row[index]
    return row.at[where_now].set(current).at[index].set(value)


def shared_layout(key):
    ndevices = N_GX * N_GZ * N_GY
    base = jax.random.fold_in(key, 4242)
    key_one, key_two, key_three, key_four = jax.random.split(base, 4)
    factor_one = jax.random.randint(key_one, (ndevices,), 0, SLOTS)
    factor_two = jax.random.randint(key_two, (ndevices,), 0, SLOTS)
    filled = 1 + factor_one * factor_two // max(SLOTS - 1, 1)
    chosen = jax.random.randint(key_three, (), 0, ndevices)
    corner_dev = (1 * N_GZ + 1) * N_GY + 1
    device_ids = jnp.arange(ndevices)
    filled = jnp.where((device_ids == chosen) | (device_ids == corner_dev), SLOTS, filled).astype(jnp.int32)
    ordering = jax.vmap(permute_region)(jax.random.split(key_four, ndevices)).astype(jnp.int32)
    first_row = place_value(ordering[0], 0, RX * RY * RZ - 1)
    ordering = ordering.at[0].set(first_row)
    corner_row = place_value(ordering[corner_dev], SLOTS - 1, 0)
    ordering = ordering.at[corner_dev].set(corner_row)
    inverse = jnp.argsort(ordering, axis=1).astype(jnp.int32)
    slot_of = jnp.where(inverse < filled[:, None], inverse, -1)
    device = jnp.arange(ndevices, dtype=jnp.int32)
    coord_y = jnp.broadcast_to((device % N_GY)[:, None], (ndevices, SLOTS))
    coord_z = jnp.broadcast_to((device // N_GY % N_GZ)[:, None], (ndevices, SLOTS))
    coord_x = jnp.broadcast_to((device // (N_GY * N_GZ))[:, None], (ndevices, SLOTS))
    position_id = ordering[:, :SLOTS]
    local_z = position_id % RZ
    local_y = position_id // RZ % RY
    local_x = position_id // (RZ * RY)
    used = jnp.arange(SLOTS)[None, :] < filled[:, None]
    region_sizes = [RX, RY, RZ]
    device_sizes = [N_GX, N_GY, N_GZ]
    columns = []
    for step_x in (-1, 0, 1):
        for step_y in (-1, 0, 1):
            for step_z in (-1, 0, 1):
                offsets = (step_x, step_y, step_z)
                if offsets == (0, 0, 0):
                    continue
                locals_now = [local_x, local_y, local_z]
                devices_now = [coord_x, coord_y, coord_z]
                present = used
                code = jnp.zeros_like(local_x)
                for axis_id in range(3):
                    if offsets[axis_id] == 0:
                        continue
                    stepped = locals_now[axis_id] + offsets[axis_id]
                    inside = (stepped >= 0) & (stepped < region_sizes[axis_id])
                    locals_now[axis_id] = stepped % region_sizes[axis_id]
                    devices_now[axis_id] = devices_now[axis_id] + jnp.where(inside, 0, offsets[axis_id])
                    code = code + jnp.where(inside, 0, 2 ** axis_id)
                    present = present & (devices_now[axis_id] >= 0) & (devices_now[axis_id] < device_sizes[axis_id])
                target_dev = (devices_now[0] * N_GZ + devices_now[2]) * N_GY + devices_now[1]
                target_dev = jnp.clip(target_dev, 0, ndevices - 1)
                target_pos = (locals_now[0] * RY + locals_now[1]) * RZ + locals_now[2]
                neighbour_slot = slot_of[target_dev, target_pos]
                encoded = jnp.where(present & (neighbour_slot >= 0), neighbour_slot + SLOTS * code, -1)
                columns.append(encoded)
    face_links = jnp.stack(columns, -1).astype(jnp.int32)
    return (filled.reshape(N_GX, N_GZ, N_GY), face_links.reshape(N_GX, N_GZ, N_GY * SLOTS, 26))


def draw_block_count(key, part):
    return shared_layout(key)[0]


def draw_neighbours(key, part):
    return shared_layout(key)[1]


def levels(key, extent, shards, smallest, largest):
    level = 1.0
    for axis_at, parts in shards:
        heights = jax.random.uniform(jax.random.fold_in(jax.random.fold_in(key, 6), axis_at), (parts,), jnp.float32, smallest / len(shards), largest / len(shards))
        level = level * jnp.repeat(jnp.exp(heights), extent[axis_at] // parts).reshape((-1,) + (1,) * (len(extent) - 1 - axis_at))
    return level


def centred(rng, dims, deviation, bound, shards=(), kind=jnp.bfloat16):
    drawn = jax.random.normal(rng, dims, jnp.float32) * deviation
    if len(shards) > 0:
        drawn = levels(rng, dims, shards, -0.22, 0.18) * drawn
    return jnp.clip(drawn, min=-bound, max=bound).astype(kind)


def setup_inputs(seed: int = 0) -> dict:
    streams_of = jax.random.split(jax.random.key(seed), 8)
    return {
        "blocks": centred(streams_of[0], (N_GX, N_GZ, N_GY * SLOTS, CIN, VOX), 1.0, 6.0, ((0, 4), (1, 4), (2, 2))),
        "block_count": draw_block_count(jax.random.fold_in(streams_of[7], 71), 0),
        "neighbours": draw_neighbours(jax.random.fold_in(streams_of[7], 71), 0),
        "conv_weight": centred(streams_of[3], (COUT, 27 * CIN), (27 * CIN) ** -0.5, 0.125),
        "conv_bias": centred(streams_of[4], (COUT,), 0.5, 3.0, (), jnp.float32),
        "head_weight": centred(streams_of[5], (COUT, COUT), COUT ** -0.5, 0.875),
        "head_bias": centred(streams_of[6], (COUT,), 0.5, 3.0, (), jnp.float32),
    }


def offset_list():
    return [(step_x, step_y, step_z) for step_x in (-1, 0, 1) for step_y in (-1, 0, 1) for step_z in (-1, 0, 1)]


def edge_piece(volume, offsets, first_axis):
    piece = volume
    for axis_id in range(3):
        dim = first_axis + axis_id
        length = piece.shape[dim]
        if offsets[axis_id] == -1:
            piece = lax.slice_in_dim(piece, length - 1, length, axis=dim)
        elif offsets[axis_id] == 1:
            piece = lax.slice_in_dim(piece, 0, 1, axis=dim)
    return piece


def assemble(pieces, first_axis):
    layers_x = []
    for step_x in (-1, 0, 1):
        layers_y = []
        for step_y in (-1, 0, 1):
            layers_y.append(jnp.concatenate([pieces[(step_x, step_y, step_z)] for step_z in (-1, 0, 1)], first_axis + 2))
        layers_x.append(jnp.concatenate(layers_y, first_axis + 1))
    return jnp.concatenate(layers_x, first_axis)


def convolve_padded(padded, conv_weight, conv_bias, head_weight, head_bias):
    channels = padded.shape[0]
    edge = padded.shape[1] - 2
    total = jnp.zeros((conv_weight.shape[0], edge * edge * edge), jnp.float32)
    for tap, offsets in enumerate(offset_list()):
        view = padded[:, 1 + offsets[0]:1 + offsets[0] + edge, 1 + offsets[1]:1 + offsets[1] + edge,
                      1 + offsets[2]:1 + offsets[2] + edge]
        total = total + jnp.dot(conv_weight[:, tap * channels:(tap + 1) * channels], view.reshape(channels, -1),
                                preferred_element_type=jnp.float32)
    hidden = jnp.maximum(total + conv_bias[:, None], 0.0).astype(jnp.bfloat16)
    mixed = jnp.dot(head_weight, hidden, preferred_element_type=jnp.float32) + head_bias[:, None]
    return mixed.astype(jnp.bfloat16)


def reference(blocks, block_count, neighbours, conv_weight, conv_bias, head_weight, head_bias):
    flat_blocks = blocks.reshape(-1, CIN, EDGE, EDGE, EDGE)
    face_links = neighbours.reshape(-1, 26)
    filled = block_count.reshape(-1)
    block_total = flat_blocks.shape[0]

    def compute_one(position):
        device = position // SLOTS
        slot_id = position % SLOTS
        coord_y = device % N_GY
        coord_z = (device // N_GY) % N_GZ
        coord_x = device // (N_GY * N_GZ)

        def active():
            volume = lax.dynamic_index_in_dim(flat_blocks, position, 0, keepdims=False)
            pieces = {(0, 0, 0): volume}
            link_index = 0
            for offsets in offset_list():
                if offsets == (0, 0, 0):
                    continue
                encoded = face_links[position, link_index]
                link_index += 1
                clean = jnp.maximum(encoded, 0)
                code = clean // SLOTS
                source_slot = clean % SLOTS
                target = [coord_x, coord_y, coord_z]
                for axis_id in range(3):
                    crossed = (code // (2 ** axis_id)) % 2
                    target[axis_id] = target[axis_id] + offsets[axis_id] * crossed
                source_dev = (target[0] * N_GZ + target[2]) * N_GY + target[1]
                source = jnp.clip(source_dev * SLOTS + source_slot, 0, block_total - 1).astype(jnp.int32)
                neighbour = lax.dynamic_index_in_dim(flat_blocks, source, 0, keepdims=False)
                face_piece = edge_piece(neighbour, offsets, 1)
                pieces[offsets] = jnp.where(encoded >= 0, face_piece, jnp.zeros_like(face_piece))
            padded = assemble(pieces, 1)
            return convolve_padded(padded, conv_weight, conv_bias, head_weight, head_bias)

        def vacant():
            return jnp.zeros((COUT, VOX), jnp.bfloat16)

        return lax.cond(slot_id < filled[device], active, vacant)

    results = lax.map(compute_one, jnp.arange(block_total, dtype=jnp.int32))
    return results.reshape(N_GX, N_GZ, N_GY * SLOTS, COUT, VOX)
```

```python
import functools

import jax
import jax.numpy as jnp
import numpy as np
from jax import lax
from jax.experimental import pallas as pl
from jax.experimental.pallas import tpu as pltpu
from jax.sharding import PartitionSpec as P

AXES = ("gx", "gy", "gz")
OFFSETS = [(a, b, c) for a in (-1, 0, 1) for b in (-1, 0, 1) for c in (-1, 0, 1)]
LINKS = [o for o in OFFSETS if o != (0, 0, 0)]
F32 = jnp.float32
BF16 = jnp.bfloat16
MESH = pl.DeviceIdType.MESH


def weight(d):
    return sum(map(abs, d))


def last(step):
    return 0 if step == -1 else 1


def far(step):
    return 15 if step == -1 else 0


KINDS = {("own", a, s): 2 * a + s for a in range(3) for s in (0, 1)}
KINDS |= {("came", a, s): 6 + 2 * a + s for a in range(3) for s in (0, 1)}
for _d in LINKS:
    if weight(_d) > 1:
        KINDS[_d] = len(KINDS)
ZERO = len(KINDS)


def entry_of(d):
    if weight(d) > 1:
        return KINDS[d]
    axis = [i for i in range(3) if d[i]][0]
    return KINDS["came", axis, last(d[axis])]


def link_tables(slots):
    entry = np.full((26, 8), ZERO * slots, np.int32)
    lane = np.zeros((26, 8), np.int32)
    for i, o in enumerate(LINKS):
        for c in range(8):
            if any(c >> a & 1 and o[a] == 0 for a in range(3)):
                continue
            e = tuple(o[a] if c >> a & 1 else 0 for a in range(3))
            if c:
                entry[i, c] = entry_of(e) * slots
            else:
                axis = [a for a in range(3) if o[a]][0]
                entry[i, c] = KINDS["own", axis, last(o[axis])] * slots
            x, y, z = (far(step) if step else 0 for step in o)
            if c == 3:
                lane[i, c] = z
            elif c in (6, 7):
                lane[i, c] = x
            elif c in (4, 5):
                lane[i, c] = y * 16 + x
            elif c == 2 or not o[0]:
                lane[i, c] = x * 16 + z
            else:
                lane[i, c] = y * 16 + z
    return np.stack([entry, lane]).reshape(2, 208)


def roll(value, shift):
    shift %= 128
    return pltpu.roll(value, shift, 1) if shift else value


def rows_of(y, cout, edge):
    lane = lax.broadcasted_iota(jnp.int32, (cout, 128), 1)
    first, final = lane < 16, lane >= 112
    down = [roll(y[0:cout, 128 * i : 128 * i + 128], 16) for i in range(y.shape[1] // 128)]
    up = [roll(y[2 * cout :, 128 * i : 128 * i + 128], -16) for i in range(y.shape[1] // 128)]
    before, after = (down[2], up[2]) if edge else (jnp.zeros_like(down[0]),) * 2
    low = y[cout : 2 * cout, 0:128] + jnp.where(first, before, down[0]) + jnp.where(final, up[1], up[0])
    high = y[cout : 2 * cout, 128:256] + jnp.where(first, down[0], down[1]) + jnp.where(final, after, up[1])
    return low, high


def exchange_kernel(
    sizes, slots, blk, cw_hbm, acc, pool, wf, planes, w, cw, gone, came, load_sem, cw_sem, send_sem, recv_sem
):
    channels = planes.shape[2] // 3
    cout = w.shape[0] // 3
    here = {axis: lax.axis_index(axis) for axis in AXES}

    def exists(d):
        ok = None
        for axis, step in zip(AXES, d):
            if step:
                at = here[axis] + step
                good = jnp.logical_and(at >= 0, at < sizes[axis])
                ok = good if ok is None else jnp.logical_and(ok, good)
        return ok

    def target(d):
        return {axis: here[axis] + step for axis, step in zip(AXES, d) if step}

    loads = [
        pltpu.make_async_copy(
            blk.at[u, :, x * 256 : x * 256 + 256],
            planes.at[u, x + 1, channels : 2 * channels, :],
            load_sem.at[u, x],
        )
        for u in range(slots)
        for x in range(16)
    ]
    weights = pltpu.make_async_copy(cw_hbm, cw, cw_sem)
    weights.start()
    barrier = pltpu.get_barrier_semaphore()
    greet = 1
    for axis in AXES:
        inner = jnp.where(here[axis] > 0, 1, 0) + jnp.where(here[axis] < sizes[axis] - 1, 1, 0)
        greet = greet * (1 + inner)
    for d in LINKS:
        @pl.when(exists(d))
        def _():
            pl.semaphore_signal(barrier, inc=1, device_id=target(d), device_id_type=MESH)
    for load in loads:
        load.start()

    def message(d):
        if d[1] and d[2]:
            return 8 + (d[1] + 1) + (d[2] + 1) // 2
        if d[1]:
            return (d[0] + 1) + (d[1] + 1) // 2
        return 4 + (d[0] + 1) + (d[2] + 1) // 2

    def own(axis, side, u):
        return KINDS["own", axis, side] * slots + u

    def copy_of(d):
        e = tuple(-step for step in d)
        at = OFFSETS.index(e)
        if weight(d) > 1:
            src, dst = gone.at[message(d)], came.at[at]
        else:
            axis = [i for i in range(3) if d[i]][0]
            into = entry_of(e) * slots
            dst = pool.at[into : into + slots]
            if axis == 0:
                x = 15 if d[0] == 1 else 0
                src = blk.at[:, :, x * 256 : x * 256 + 256]
            else:
                kept = own(axis, last(-d[axis]), 0)
                src = pool.at[kept : kept + slots]
        return pltpu.make_async_remote_copy(
            src_ref=src,
            dst_ref=dst,
            send_sem=send_sem.at[at],
            recv_sem=recv_sem.at[at],
            device_id=target(d),
            device_id_type=MESH,
        )

    def start(d):
        @pl.when(exists(d))
        def _():
            copy_of(d).start()

    pl.semaphore_wait(barrier, greet - 1)
    for d in LINKS:
        if weight(d) == 1 and d[0]:
            start(d)
    for load in loads:
        load.wait()

    lane = lax.broadcasted_iota(jnp.int32, (channels, 128), 1)
    group, place = lane // 16, lane % 16
    third = channels // 3
    cut = lax.broadcasted_iota(jnp.int32, (third, 128), 1)
    cut_group, cut_place = cut // 16, cut % 16

    def tile(u, x, half):
        return planes[u, x + 1, channels : 2 * channels, half * 128 : half * 128 + 128]

    def runs(at, piece):
        made = None
        for part in range(3):
            for u in range(slots):
                value, lies = piece(u, part)
                goes = part * slots + u
                moved = roll(value, (goes - lies) * 16)
                made = moved if made is None else jnp.where(cut_group == goes, moved, made)
        gone[at] = made

    for d in LINKS:
        if d[0] and d[1] and not d[2]:
            x, half = (15 if d[0] == 1 else 0), (1 if d[1] == 1 else 0)

            def strip(u, part):
                c = channels + part * third
                return planes[u, x + 1, c : c + third, half * 128 : half * 128 + 128], 7 * half

            runs(message(d), strip)
            start(d)
    for dz in (1, -1):
        side = last(-dz)
        for u in range(slots):
            for half in (0, 1):
                made = None
                for x in range(16):
                    moved = roll(tile(u, x, half), x - 15 if side == 0 else x)
                    made = moved if made is None else jnp.where(place == x, moved, made)
                pool[own(2, side, u), :, half * 128 : half * 128 + 128] = made
        start((0, 0, dz))
        for dx in (1, -1):
            d = (dx, 0, dz)
            made = None
            for part in range(3):
                for u in range(slots):
                    for half in (0, 1):
                        goes = (part * slots + u) * 2 + half
                        value = pool[own(2, side, u), part * third : part * third + third, half * 128 : half * 128 + 128]
                        moved = roll(value, goes - (15 if dx == 1 else 0))
                        made = moved if made is None else jnp.where(cut_place == goes, moved, made)
            gone[message(d)] = made
            start(d)
        for dy in (1, -1):
            half = 1 if dy == 1 else 0

            def line(u, part):
                return pool[own(2, side, u), part * third : part * third + third, half * 128 : half * 128 + 128], 7 * half

            runs(message((0, dy, dz)), line)
            for dx in (0, 1, -1):
                start((dx, dy, dz))
    for side in (0, 1):
        for u in range(slots):
            for half in (0, 1):
                made = None
                for k in range(8):
                    moved = roll(tile(u, half * 8 + k, 1 - side), k * 16 - (112 if side == 0 else 0))
                    made = moved if made is None else jnp.where(group == k, moved, made)
                pool[own(1, side, u), :, half * 128 : half * 128 + 128] = made
        start((0, 1 if side == 0 else -1, 0))

    for u in range(slots):
        pool[own(0, 0, u)] = planes[u, 16, channels : 2 * channels, :]
        pool[own(0, 1, u)] = planes[u, 1, channels : 2 * channels, :]
        pool[ZERO * slots + u] = jnp.zeros(pool.shape[1:], pool.dtype)
        for end in (0, 17):
            planes[u, end] = jnp.zeros(planes.shape[2:], planes.dtype)
    weights.wait()
    depth = 3 * channels
    for a in range(3):
        for b in range(3):
            at = (a * 9 + b * 3) * channels
            taps = cw[:, at : at + depth]
            w[b * cout : (b + 1) * cout, a * depth : (a + 1) * depth] = taps
            if a != 1:
                wf[last(a - 1), b * cout : (b + 1) * cout, :] = taps
            if b != 1:
                wf[2 + last(b - 1), a * cout : (a + 1) * cout, :] = taps
            for k in (0, 2):
                wf[4 + k // 2, b * cout : (b + 1) * cout, a * channels : (a + 1) * channels] = taps[
                    :, k * channels : (k + 1) * channels
                ]

    def build(u, p):
        for half in (0, 1):
            lanes = slice(128 * half, 128 * half + 128)
            value = planes[u, p, channels : 2 * channels, lanes]
            for dz in (-1, 1):
                moved = jnp.where(place == (0 if dz == -1 else 15), jnp.zeros_like(value), roll(value, -dz))
                planes[u, p, (dz + 1) * channels : (dz + 2) * channels, lanes] = moved

    def per_slot(u, _):
        build(u, 1)
        for x in range(16):
            if x < 15:
                build(u, x + 2)
            y = jnp.dot(w[...], planes[u, x : x + 3].reshape(3 * depth, 256), preferred_element_type=F32)
            acc[u, x, :, 0:128], acc[u, x, :, 128:256] = rows_of(y, cout, False)
        return 0

    lax.fori_loop(0, slots, per_slot, 0)

    for d in sorted(LINKS, key=lambda d: -weight(d)):
        e = tuple(-step for step in d)

        @pl.when(exists(e))
        def _():
            copy_of(d).wait_recv()
            if weight(d) == 1:
                return
            base = KINDS[e] * slots
            for u in range(slots):
                for part in range(3):
                    rows = slice(part * third, part * third + third)
                    got = came[OFFSETS.index(e)]
                    if d[1]:
                        pool[base + u, rows, 0:128] = roll(got, -16 * (part * slots + u))
                    else:
                        for half in (0, 1):
                            lies = (part * slots + u) * 2 + half
                            pool[base + u, rows, half * 128 : half * 128 + 128] = roll(got, far(e[0]) - lies)
    for d in LINKS:
        @pl.when(exists(d))
        def _():
            copy_of(d).wait_send()


def finish_kernel(slots, count, links, table, acc, pool, wf, cb, hw, hb, out, stack, faces, made, out_sem):
    channels = pool.shape[1]
    cout = hw.shape[0]
    eye = lax.broadcasted_iota(jnp.int32, (cout, cout), 0) == lax.broadcasted_iota(jnp.int32, (cout, cout), 1)

    def column(ref):
        return jnp.sum(jnp.where(eye, ref[...], 0.0), axis=1, keepdims=True)

    bias, head_bias = column(cb), column(hb)
    lane = lax.broadcasted_iota(jnp.int32, (channels, 128), 1)
    group, place = lane // 16, lane % 16
    lane_out = lax.broadcasted_iota(jnp.int32, (cout, 128), 1)
    group_out, place_out = lane_out // 16, lane_out % 16

    def link(s, o):
        return links[s, LINKS.index(o)]

    def entry_for(s, o, codes):
        v = link(s, o)
        c = jnp.maximum(v, 0) // slots
        found = functools.reduce(jnp.logical_or, [c == k for k in codes])
        found = jnp.logical_and(v >= 0, found)
        return jnp.where(found, table[0, LINKS.index(o) * 8 + c] + v % slots, ZERO * slots), c

    def has(s, o, codes):
        v = link(s, o)
        return jnp.logical_and(v >= 0, functools.reduce(jnp.logical_or, [v // slots == k for k in codes]))

    def fetch(s, o, codes, goes):
        entry, c = entry_for(s, o, codes)
        lies = table[1, LINKS.index(o) * 8 + c]
        half = lies // 128
        got = pool[entry, :, pl.ds(pl.multiple_of(half * 128, 128), 128)]
        return pltpu.roll(got, lax.rem(goes - lies + 256, 128), 1)

    def face(s, axis, step):
        def off(**steps):
            return tuple(steps.get(name, 0) for name in "xyz")

        name = "xyz"[axis]
        column_axis = "x" if axis == 2 else "z"
        row_axis = {0: "y", 1: None, 2: "y"}[axis]
        plain = {0: (0, 1), 1: (0, 2), 2: (0, 4)}[axis]
        edge = {0: (0, 1), 1: (0, 2), 2: (4, 5)}[axis]
        row_codes = {0: (0, 1, 2, 3), 1: (), 2: (4, 6)}[axis]
        parts = [(off(**{name: step}), plain)]
        parts += [(off(**{name: step, column_axis: e}), edge) for e in (-1, 1)]
        if row_axis:
            parts += [(off(**{name: step, row_axis: r}), row_codes) for r in (-1, 1)]
        if axis == 0:
            parts += [(off(x=step, y=r, z=e), tuple(range(8))) for r in (-1, 1) for e in (-1, 1)]
        active = functools.reduce(jnp.logical_or, [has(s, o, codes) for o, codes in parts])

        def work():
            centre, _c = entry_for(s, *parts[0])
            for half in (0, 1):
                lanes = slice(half * 128, half * 128 + 128)
                value = pool[centre, :, lanes]
                stack[channels : 2 * channels, lanes] = value
                for e in (-1, 1):
                    entry, _c = entry_for(s, *parts[1 + (e + 1) // 2])
                    at = 0 if e == -1 else 15
                    piece = roll(pool[entry, :, lanes], 15 * e)
                    stack[(e + 1) * channels : (e + 2) * channels, lanes] = jnp.where(
                        place == at, piece, roll(value, -e)
                    )
            if row_axis:
                line = None
                for r in (-1, 1):
                    o, codes = parts[3 + (r + 1) // 2]
                    got = fetch(s, o, codes, 112 if r == -1 else 0)
                    line = got if line is None else jnp.where(group == 0, got, line)
                stack[channels : 2 * channels, 256:384] = line
                for e in (-1, 1):
                    moved = roll(line, -e)
                    at = 0 if e == -1 else 15
                    if axis == 0:
                        for r in (-1, 1):
                            goes = (112 if r == -1 else 0) + at
                            got = fetch(s, off(x=step, y=r, z=e), tuple(range(8)), goes)
                            moved = jnp.where(lane == goes, got, moved)
                    else:
                        moved = jnp.where(place == at, jnp.zeros_like(moved), moved)
                    stack[(e + 1) * channels : (e + 2) * channels, 256:384] = moved
            wide = 384 if row_axis else 256
            y = jnp.dot(wf[2 * axis + last(step)], stack[:, 0:wide], preferred_element_type=F32)
            low, high = rows_of(y, cout, bool(row_axis))
            faces[2 * axis + last(step), :, 0:128] = low
            faces[2 * axis + last(step), :, 128:256] = high

        def none():
            faces[2 * axis + last(step)] = jnp.zeros(faces.shape[1:], F32)

        pl.when(active)(work)
        pl.when(jnp.logical_not(active))(none)
        return active

    def head(s, x, low, high):
        hidden = jnp.concatenate([jnp.maximum(v + bias, 0.0).astype(BF16) for v in (low, high)], 1)
        mixed = jnp.dot(hw[...], hidden, preferred_element_type=F32) + head_bias
        made[s, :, x * 256 : x * 256 + 256] = mixed.astype(made.dtype)

    copies = []
    for s in range(slots):
        used = s < count[0]

        @pl.when(used)
        def _():
            for step in (-1, 1):
                face(s, 0, step)
            sides = [face(s, axis, step) for axis in (1, 2) for step in (-1, 1)]
            any_side = functools.reduce(jnp.logical_or, sides)

            def planes(with_sides):
                for x in range(16):
                    halves = []
                    for half in (0, 1):
                        lanes = slice(half * 128, half * 128 + 128)
                        v = acc[s, x, :, lanes]
                        if x in (0, 15):
                            v = v + faces[x // 15, :, lanes]
                        if with_sides:
                            goes = 7 if half else 0
                            near = faces[2 + half, :, (x // 8) * 128 : (x // 8) * 128 + 128]
                            v = v + jnp.where(group_out == goes, roll(near, (goes - x % 8) * 16), 0.0)
                            v = v + jnp.where(place_out == 0, roll(faces[4, :, lanes], -x), 0.0)
                            v = v + jnp.where(place_out == 15, roll(faces[5, :, lanes], 15 - x), 0.0)
                        halves.append(v)
                    head(s, x, *halves)

            pl.when(any_side)(lambda: planes(True))
            pl.when(jnp.logical_not(any_side))(lambda: planes(False))

        @pl.when(jnp.logical_not(used))
        def _():
            made[s] = jnp.zeros(made.shape[1:], made.dtype)

        copies.append(pltpu.make_async_copy(made.at[s], out.at[s], out_sem.at[s]))
        copies[-1].start()
    for copy in copies:
        copy.wait()


def body(sizes, blocks, block_count, neighbours, conv_weight, conv_bias, head_weight, head_bias):
    slots, channels, voxels = blocks.shape[2:]
    cout = head_weight.shape[0]
    blk = blocks.reshape(slots, channels, voxels)
    vmem = pl.BlockSpec(memory_space=pltpu.VMEM)
    smem = pl.BlockSpec(memory_space=pltpu.SMEM)
    hbm = pl.BlockSpec(memory_space=pltpu.HBM)
    acc, pool, wf = pl.pallas_call(
        functools.partial(exchange_kernel, sizes, slots),
        out_shape=[
            jax.ShapeDtypeStruct((slots, 16, cout, 256), F32),
            jax.ShapeDtypeStruct(((ZERO + 1) * slots, channels, 256), blocks.dtype),
            jax.ShapeDtypeStruct((6, 3 * cout, 3 * channels), BF16),
        ],
        in_specs=[hbm, hbm],
        out_specs=[vmem] * 3,
        scratch_shapes=[
            pltpu.VMEM((slots, 18, 3 * channels, 256), BF16),
            pltpu.VMEM((3 * cout, 9 * channels), BF16),
            pltpu.VMEM(conv_weight.shape, BF16),
            pltpu.VMEM((12, channels // 3, 128), BF16),
            pltpu.VMEM((27, channels // 3, 128), BF16),
            pltpu.SemaphoreType.DMA((slots, 16)),
            pltpu.SemaphoreType.DMA,
            pltpu.SemaphoreType.DMA((27,)),
            pltpu.SemaphoreType.DMA((27,)),
        ],
        compiler_params=pltpu.CompilerParams(collective_id=0, has_side_effects=True, vmem_limit_bytes=24 << 20),
        name="exchange",
    )(pltpu.with_memory_space_constraint(blk, pltpu.HBM), pltpu.with_memory_space_constraint(conv_weight, pltpu.HBM))
    out = pl.pallas_call(
        functools.partial(finish_kernel, slots),
        out_shape=jax.ShapeDtypeStruct((slots, cout, voxels), BF16),
        in_specs=[smem] * 3 + [vmem] * 6,
        out_specs=hbm,
        scratch_shapes=[
            pltpu.VMEM((3 * channels, 384), BF16),
            pltpu.VMEM((6, cout, 256), F32),
            pltpu.VMEM((slots, cout, voxels), BF16),
            pltpu.SemaphoreType.DMA((slots,)),
        ],
        compiler_params=pltpu.CompilerParams(vmem_limit_bytes=20 << 20),
        name="finish",
    )(
        block_count.reshape(1),
        neighbours.reshape(slots, 26),
        jnp.asarray(link_tables(slots)),
        acc,
        pool,
        wf,
        conv_bias[None],
        head_weight,
        head_bias[None],
    )
    return out.reshape(1, 1, slots, cout, voxels)


def solution(mesh):
    placed = (
        P("gx", "gz", "gy", None, None),
        P("gx", "gz", "gy"),
        P("gx", "gz", "gy", None),
        P(),
        P(),
        P(),
        P(),
    )
    return jax.shard_map(
        functools.partial(body, dict(mesh.shape)),
        mesh=mesh,
        in_specs=placed,
        out_specs=P("gx", "gz", "gy", None, None),
        check_vma=False,
    )
```

```python
import functools

import jax
import jax.numpy as jnp
import numpy as np
from jax import lax
from jax.experimental import pallas as pl
from jax.experimental.pallas import tpu as pltpu
from jax.sharding import PartitionSpec as P

AXES = ("gx", "gy", "gz")
OFFSETS = [(a, b, c) for a in (-1, 0, 1) for b in (-1, 0, 1) for c in (-1, 0, 1)]
LINKS = [o for o in OFFSETS if o != (0, 0, 0)]
F32 = jnp.float32
BF16 = jnp.bfloat16
MESH = pl.DeviceIdType.MESH


def weight(d):
    return sum(map(abs, d))


def last(step):
    return 0 if step == -1 else 1


def far(step):
    return 15 if step == -1 else 0


KINDS = {("own", a, s): 2 * a + s for a in range(3) for s in (0, 1)}
KINDS |= {("came", a, s): 6 + 2 * a + s for a in range(3) for s in (0, 1)}
for _d in LINKS:
    if weight(_d) > 1:
        KINDS[_d] = len(KINDS)
ZERO = len(KINDS)


def entry_of(d):
    if weight(d) > 1:
        return KINDS[d]
    axis = [i for i in range(3) if d[i]][0]
    return KINDS["came", axis, last(d[axis])]


def piece_of(o, c):
    e = tuple(o[a] if c >> a & 1 else 0 for a in range(3))
    if c:
        kind = entry_of(e)
    else:
        axis = [a for a in range(3) if o[a]][0]
        kind = KINDS["own", axis, last(o[axis])]
    x, y, z = (far(step) if step else 0 for step in o)
    if c == 7:
        lane = 0
    elif c == 3:
        lane = z
    elif c in (4, 5):
        lane = y * 16 + x
    elif c in (2, 6) or not o[0]:
        lane = x * 16 + z
    else:
        lane = y * 16 + z
    return kind, lane


PARTS = 9
FACE, SIDE, RING = 0, 1, 2


def face_parts(axis, step):
    def off(**steps):
        return tuple(steps.get(name, 0) for name in "xyz")

    name = "xyz"[axis]
    parts = [(off(**{name: step}), {0: (0, 1), 1: (0, 2), 2: (0, 4)}[axis])]
    for e in (-1, 1):
        parts.append((off(**{name: step, "x" if axis == 2 else "z": e}), {0: (0, 1), 1: (0, 2, 6), 2: (4, 5)}[axis]))
    for r in (-1, 1):
        if axis == 1:
            parts.append((off(y=step), ()))
        else:
            parts.append((off(**{name: step, "y": r}), {0: (0, 1, 2, 3), 2: (4,)}[axis]))
    for e in (-1, 1):
        for r in (-1, 1):
            parts.append((off(x=step, y=r, z=e), tuple(range(8))) if axis == 0 else (off(**{name: step}), ()))
    return parts


def plan(slots):
    entry = np.full((8, 128), -1, np.int32)
    lane = np.zeros((8, 128), np.int32)
    pick = np.zeros((32, 128), np.int32)
    needs = np.zeros((128, 128), np.int32)
    for f in range(6):
        for k, (o, codes) in enumerate(face_parts(f // 2, (-1, 1)[f % 2])):
            j = f * PARTS + k
            pick[LINKS.index(o), j] = 1
            for c in codes:
                if any(c >> a & 1 and o[a] == 0 for a in range(3)):
                    continue
                kind, at = piece_of(o, c)
                entry[c, j], lane[c, j] = kind * slots, at
            needs[j, FACE] = 1
            needs[j, SIDE] = f >= 2
            needs[j, RING + f // 2] = k >= 3
    return np.concatenate([entry, lane, pick, needs])


def roll(value, shift):
    shift %= 128
    return pltpu.roll(value, shift, 1) if shift else value


def rows_of(y, cout):
    lane = lax.broadcasted_iota(jnp.int32, (cout, 128), 1)
    first, final = lane < 16, lane >= 112
    down = [roll(y[0:cout, at : at + 128], 16) for at in (0, 128)]
    up = [roll(y[2 * cout :, at : at + 128], -16) for at in (0, 128)]
    zero = jnp.zeros_like(down[0])
    low = y[cout : 2 * cout, 0:128] + jnp.where(first, zero, down[0]) + jnp.where(final, up[1], up[0])
    high = y[cout : 2 * cout, 128:256] + jnp.where(first, down[0], down[1]) + jnp.where(final, zero, up[1])
    return low, high


def exchange_kernel(
    sizes, slots, blk_hbm, cw_hbm, links_hbm, plan_hbm, cb_hbm, hb_hbm, acc, pool, wf, meta, bias,
    blk, planes, w, cw, links, table, biases, gone, came, load_sem, aux_sem, send_sem, recv_sem,
):
    channels = blk.shape[1]
    cout = w.shape[0] // 3
    here = {axis: lax.axis_index(axis) for axis in AXES}

    def exists(d):
        ok = None
        for axis, step in zip(AXES, d):
            if step:
                at = here[axis] + step
                good = jnp.logical_and(at >= 0, at < sizes[axis])
                ok = good if ok is None else jnp.logical_and(ok, good)
        return ok

    def target(d):
        return {axis: here[axis] + step for axis, step in zip(AXES, d) if step}

    partners = [d for d in LINKS if not d[1] or weight(d) == 1]
    messages = [d for d in LINKS if weight(d) < 3]
    span = blk.shape[2] // 2
    loads = [
        pltpu.make_async_copy(
            blk_hbm.at[u, :, k * span : k * span + span], blk.at[u, :, k * span : k * span + span], load_sem.at[u, k]
        )
        for u in range(slots)
        for k in (0, 1)
    ]
    barrier = pltpu.get_barrier_semaphore()
    for d in partners:
        @pl.when(exists(d))
        def _():
            pl.semaphore_signal(barrier, inc=1, device_id=target(d), device_id_type=MESH)
    for load in loads:
        load.start()
    others = [
        pltpu.make_async_copy(src, dst, aux_sem.at[i])
        for i, (src, dst) in enumerate([(cw_hbm, cw), (links_hbm, links), (plan_hbm, table), (cb_hbm, biases.at[0:1]), (hb_hbm, biases.at[1:2])])
    ]
    for other in others:
        other.start()
    near = {
        axis: jnp.where(here[axis] > 0, 1, 0) + jnp.where(here[axis] < sizes[axis] - 1, 1, 0) for axis in AXES
    }

    def own(axis, side, u):
        return KINDS["own", axis, side] * slots + u

    def copy_of(d):
        to = d if weight(d) == 1 else (d[0], 0, d[2])
        e = (-to[0], d[1] if weight(d) > 1 else -d[1], -to[2])
        if weight(d) > 1:
            src, dst = gone.at[OFFSETS.index(d)], came.at[OFFSETS.index(e)]
        else:
            axis = [i for i in range(3) if d[i]][0]
            into = entry_of(e) * slots
            dst = pool.at[into : into + slots]
            if axis == 0:
                x = 15 if d[0] == 1 else 0
                src = blk_hbm.at[:, :, x * 256 : x * 256 + 256]
            else:
                kept = own(axis, last(-d[axis]), 0)
                src = pool.at[kept : kept + slots]
        return pltpu.make_async_remote_copy(
            src_ref=src,
            dst_ref=dst,
            send_sem=send_sem.at[OFFSETS.index(d)],
            recv_sem=recv_sem.at[OFFSETS.index(e)],
            device_id=target(to),
            device_id_type=MESH,
        )

    def start(d):
        @pl.when(exists(d))
        def _():
            copy_of(d).start()

    def sender(e):
        return (-e[0], e[1] if weight(e) > 1 else -e[1], -e[2])

    pl.semaphore_wait(barrier, (1 + near["gx"]) * (1 + near["gz"]) - 1 + near["gy"])
    start((1, 0, 0))
    start((-1, 0, 0))
    for load in loads:
        load.wait()

    lane = lax.broadcasted_iota(jnp.int32, (channels, 128), 1)
    group, place = lane // 16, lane % 16
    third = channels // 3
    cut = lax.broadcasted_iota(jnp.int32, (third, 128), 1)
    cut_group, cut_place = cut // 16, cut % 16

    def tile(u, x, half):
        at = x * 256 + half * 128
        return blk[u, :, at : at + 128]

    def third_of(entry, part, half):
        return pool[entry, part * third : part * third + third, half * 128 : half * 128 + 128]

    for side in (0, 1):
        for u in range(slots):
            for half in (0, 1):
                made = None
                for k in range(8):
                    moved = roll(tile(u, half * 8 + k, 1 - side), k * 16 - (112 if side == 0 else 0))
                    made = moved if made is None else jnp.where(group == k, moved, made)
                pool[own(1, side, u), :, half * 128 : half * 128 + 128] = made
        start((0, 1 if side == 0 else -1, 0))
    for dz in (1, -1):
        side = last(-dz)
        for u in range(slots):
            for half in (0, 1):
                made = None
                for x in range(16):
                    moved = roll(tile(u, x, half), x - 15 if side == 0 else x)
                    made = moved if made is None else jnp.where(place == x, moved, made)
                pool[own(2, side, u), :, half * 128 : half * 128 + 128] = made
        start((0, 0, dz))

    for u in range(slots):
        pool[own(0, 0, u)] = blk[u, :, 15 * 256 : 16 * 256]
        pool[own(0, 1, u)] = blk[u, :, 0:256]
        pool[ZERO * slots + u] = jnp.zeros(pool.shape[1:], pool.dtype)
        for end in (0, 17):
            planes[u, end] = jnp.zeros(planes.shape[2:], planes.dtype)

    def strips(d, entry, col):
        made = None
        for part in range(3):
            for u in range(slots):
                for half in (0, 1):
                    goes = (part * slots + u) * 2 + half
                    moved = roll(third_of(entry(u), part, half), goes - col)
                    made = moved if made is None else jnp.where(cut_place == goes, moved, made)
        return made

    def corner_lane(dy, u, part):
        return part * 16 + 12 + last(dy) * slots + u

    for dy in (-1, 1):
        @pl.when(exists((0, dy, 0)))
        def _():
            copy_of((0, -dy, 0)).wait_recv()
    for dy in (-1, 1):
        @pl.when(exists((0, dy, 0)))
        def _():
            def entry(u):
                return KINDS["came", 1, last(dy)] * slots + u

            for dx in (1, -1):
                made = None
                for part in range(3):
                    for u in range(slots):
                        goes = part * slots + u
                        half = 1 if dx == 1 else 0
                        moved = roll(third_of(entry(u), part, half), (goes - 7 * half) * 16)
                        made = moved if made is None else jnp.where(cut_group == goes, moved, made)
                gone[OFFSETS.index((dx, dy, 0))] = made
                start((dx, dy, 0))
            for dz in (1, -1):
                gone[OFFSETS.index((0, dy, dz))] = strips((0, dy, dz), entry, 15 if dz == 1 else 0)
                start((0, dy, dz))
    for dx in (1, -1):
        for dz in (1, -1):
            x, z = (15 if dx == 1 else 0), (15 if dz == 1 else 0)
            made = strips((dx, 0, dz), lambda u: own(2, last(-dz), u), x)
            for dy in (-1, 1):
                for u in range(slots):
                    for part in range(3):
                        goes = corner_lane(dy, u, part)
                        half = x // 8
                        moved = roll(
                            third_of(KINDS["came", 1, last(dy)] * slots + u, part, half), goes - (x * 16 + z) % 128
                        )
                        made = jnp.where(cut == goes, moved, made)
            gone[OFFSETS.index((dx, 0, dz))] = made
            start((dx, 0, dz))

    others[0].wait()
    depth = 3 * channels
    for a in range(3):
        for b in range(3):
            at = (a * 9 + b * 3) * channels
            taps = cw[:, at : at + depth]
            w[b * cout : (b + 1) * cout, a * depth : (a + 1) * depth] = taps
            if a != 1:
                wf[last(a - 1), b * cout : (b + 1) * cout, :] = taps
            if b != 1:
                wf[2 + last(b - 1), a * cout : (a + 1) * cout, :] = taps
            for k in (0, 2):
                wf[4 + k // 2, b * cout : (b + 1) * cout, a * channels : (a + 1) * channels] = taps[
                    :, k * channels : (k + 1) * channels
                ]

    def build(u, p):
        for half in (0, 1):
            lanes = slice(128 * half, 128 * half + 128)
            value = blk[u, :, (p - 1) * 256 + 128 * half : (p - 1) * 256 + 128 * half + 128]
            planes[u, p, channels : 2 * channels, lanes] = value
            for dz in (-1, 1):
                moved = jnp.where(place == (0 if dz == -1 else 15), jnp.zeros_like(value), roll(value, -dz))
                planes[u, p, (dz + 1) * channels : (dz + 2) * channels, lanes] = moved

    def per_slot(u, _):
        build(u, 1)
        for x in range(16):
            if x < 15:
                build(u, x + 2)
            y = jnp.dot(w[...], planes[u, x : x + 3].reshape(3 * depth, 256), preferred_element_type=F32)
            acc[u, x, :, 0:128], acc[u, x, :, 128:256] = rows_of(y, cout)
        return 0

    lax.fori_loop(0, slots, per_slot, 0)

    for other in others[1:]:
        other.wait()
    value = jnp.dot(links[...].astype(F32), table[16 : 16 + links.shape[1], :].astype(F32), preferred_element_type=F32)
    value = value.astype(jnp.int32)
    code, slot = value >> 1, value & 1
    entry, lies = jnp.full_like(value, -1), jnp.zeros_like(value)
    for c in range(8):
        entry = jnp.where(code == c, table[c : c + 1, :], entry)
        lies = jnp.where(code == c, table[8 + c : 9 + c, :], lies)
    needed = jnp.dot(
        jnp.where(entry >= 0, 1.0, 0.0), table[48:176, :].astype(F32), preferred_element_type=F32
    ).astype(jnp.int32)
    meta[0:slots, :] = jnp.where(entry >= 0, entry + slot, ZERO * slots)
    meta[slots : 2 * slots, :] = lies
    meta[2 * slots : 3 * slots, :] = needed
    eye = lax.broadcasted_iota(jnp.int32, (cout, cout), 0) == lax.broadcasted_iota(jnp.int32, (cout, cout), 1)
    for i in (0, 1):
        column = jnp.sum(jnp.where(eye, biases[i : i + 1, :], 0.0), axis=1, keepdims=True)
        bias[i] = jnp.zeros(bias.shape[1:], F32) + column

    for e in sorted(messages, key=lambda e: -weight(e)):
        @pl.when(exists(e))
        def _():
            if weight(e) > 1 or not e[1]:
                copy_of(sender(e)).wait_recv()
            if weight(e) == 1:
                return
            got = came[OFFSETS.index(e)]
            for u in range(slots):
                for part in range(3):
                    rows = slice(part * third, part * third + third)
                    if not e[2]:
                        pool[KINDS[e] * slots + u, rows, 0:128] = roll(got, -16 * (part * slots + u))
                        continue
                    for half in (0, 1):
                        lies = (part * slots + u) * 2 + half
                        col = far(e[2] if e[1] else e[0])
                        pool[KINDS[e] * slots + u, rows, half * 128 : half * 128 + 128] = roll(got, col - lies)
                    if not e[1]:
                        for dy in (-1, 1):
                            pool[KINDS[e[0], dy, e[2]] * slots + u, rows, 0:128] = roll(got, -corner_lane(dy, u, part))
    for d in messages:
        @pl.when(exists(d))
        def _():
            copy_of(d).wait_send()


def finish_kernel(slots, meta, count, acc, pool, wf, bias, hw, out, stack, ring, faces, made, out_sem):
    channels = pool.shape[1]
    cout = hw.shape[0]
    lane = lax.broadcasted_iota(jnp.int32, (channels, 128), 1)
    group, place = lane // 16, lane % 16
    lane_out = lax.broadcasted_iota(jnp.int32, (cout, 128), 1)
    group_out, place_out = lane_out // 16, lane_out % 16
    at_ends = jnp.logical_or(place_out == 0, place_out == 15)
    row_bias, head_bias = bias[0], bias[1]
    both_head = jnp.concatenate([head_bias, head_bias], 1)

    def entry(s, f, k):
        return meta[s, f * PARTS + k]

    def fetch(s, f, k, goes):
        lies = meta[slots + s, f * PARTS + k]
        got = pool[entry(s, f, k), :, pl.ds(pl.multiple_of((lies // 128) * 128, 128), 128)]
        return pltpu.roll(got, lax.rem(goes - lies + 256, 128), 1)

    def face(s, f):
        for half in (0, 1):
            lanes = slice(half * 128, half * 128 + 128)
            value = pool[entry(s, f, 0), :, lanes]
            stack[f, channels : 2 * channels, lanes] = value
            for e in (-1, 1):
                at = 0 if e == -1 else 15
                piece = roll(pool[entry(s, f, 1 + last(e)), :, lanes], 15 * e)
                stack[f, (e + 1) * channels : (e + 2) * channels, lanes] = jnp.where(
                    place == at, piece, roll(value, -e)
                )
        y = jnp.dot(wf[f], stack[f], preferred_element_type=F32)
        faces[f, :, 0:128], faces[f, :, 128:256] = rows_of(y, cout)

    def rings(s, axis):
        line = None
        for i in (0, 1):
            for r in (0, 1):
                goes = 1 - i if r else 6 + i
                got = fetch(s, 2 * axis + i, 3 + r, goes * 16)
                line = got if line is None else jnp.where(group == goes, got, line)
        ring[channels : 2 * channels, :] = line
        for e in (-1, 1):
            at = 0 if e == -1 else 15
            moved = jnp.where(place == at, jnp.zeros_like(line), roll(line, -e))
            if axis == 0:
                for i in (0, 1):
                    for r in (0, 1):
                        goes = (1 - i if r else 6 + i) * 16 + at
                        moved = jnp.where(lane == goes, fetch(s, i, 5 + 2 * last(e) + r, goes), moved)
            ring[(e + 1) * channels : (e + 2) * channels, :] = moved
        for i in (0, 1):
            f = 2 * axis + i
            y = jnp.dot(wf[f], ring[...], preferred_element_type=F32)
            faces[f, :, 0:128] += jnp.where(group_out == 0, roll(y[0:cout], 32 - 16 * i), 0.0)
            faces[f, :, 128:256] += jnp.where(group_out == 7, roll(y[2 * cout :], -32 + 16 * i), 0.0)

    def plane(s, x, keep, with_faces, with_sides):
        hidden = []
        for half in (0, 1):
            lanes = slice(half * 128, half * 128 + 128)
            v = acc[s, x, :, lanes] + row_bias
            if with_faces and x in (0, 15):
                v = v + faces[x // 15, :, lanes]
            if with_sides:
                goes = 7 if half else 0
                strip = faces[2 + half, :, (x // 8) * 128 : (x // 8) * 128 + 128]
                v = v + jnp.where(group_out == goes, roll(strip, (goes - x % 8) * 16), 0.0)
                ends = jnp.where(place_out == x, faces[4, :, lanes], faces[5, :, lanes])
                v = v + jnp.where(at_ends, roll(ends, -x), 0.0)
            hidden.append(jnp.maximum(v, 0.0).astype(BF16))
        mixed = jnp.dot(hw[...], jnp.concatenate(hidden, 1), preferred_element_type=F32) + both_head
        made[s, :, x * 256 : x * 256 + 256] = (mixed * keep).astype(made.dtype)

    def chunk(s, q):
        lanes = pl.ds(q * 1024, 1024)
        return pltpu.make_async_copy(made.at[s, :, lanes], out.at[s, :, lanes], out_sem.at[s, q])

    def per_slot(s, _):
        keep = jnp.where(s < count[0, 0, 0], 1.0, 0.0)
        any_face = meta[2 * slots + s, FACE] > 0
        any_side = meta[2 * slots + s, SIDE] > 0

        @pl.when(any_face)
        def _():
            for f in range(6):
                face(s, f)
            for axis in (0, 2):
                pl.when(meta[2 * slots + s, RING + axis] > 0)(functools.partial(rings, s, axis))

        def run(with_faces, with_sides):
            if with_sides:
                for half in (0, 1):
                    lanes = slice(half * 128, half * 128 + 128)
                    faces[5, :, lanes] = roll(faces[5, :, lanes], 15)
            for q in range(4):
                for k in range(4):
                    plane(s, q * 4 + k, keep, with_faces, with_sides)
                chunk(s, q).start()

        pl.when(any_side)(lambda: run(True, True))
        pl.when(jnp.logical_and(any_face, jnp.logical_not(any_side)))(lambda: run(True, False))
        pl.when(jnp.logical_not(any_face))(lambda: run(False, False))
        return 0

    lax.fori_loop(0, slots, per_slot, 0)
    for s in range(slots):
        for q in range(4):
            chunk(s, q).wait()


def finish(slots, voxels, meta, block_count, acc, pool, wf, bias, head_weight):
    channels = pool.shape[1]
    cout = head_weight.shape[0]
    return pl.pallas_call(
        functools.partial(finish_kernel, slots),
        out_shape=jax.ShapeDtypeStruct((slots, cout, voxels), BF16),
        in_specs=[pl.BlockSpec(memory_space=pltpu.SMEM)] * 2 + [pl.BlockSpec(memory_space=pltpu.VMEM)] * 5,
        out_specs=pl.BlockSpec(memory_space=pltpu.HBM),
        scratch_shapes=[
            pltpu.VMEM((6, 3 * channels, 256), BF16),
            pltpu.VMEM((3 * channels, 128), BF16),
            pltpu.VMEM((6, cout, 256), F32),
            pltpu.VMEM((slots, cout, voxels), BF16),
            pltpu.SemaphoreType.DMA((slots, 4)),
        ],
        compiler_params=pltpu.CompilerParams(vmem_limit_bytes=20 << 20),
        name="finish",
    )(meta, block_count, acc, pool, wf, bias, head_weight)


def body(sizes, blocks, block_count, neighbours, conv_weight, conv_bias, head_weight, head_bias):
    slots, channels, voxels = blocks.shape[2:]
    cout = head_weight.shape[0]
    vmem = pl.BlockSpec(memory_space=pltpu.VMEM)
    hbm = pl.BlockSpec(memory_space=pltpu.HBM)
    table = jnp.asarray(plan(slots))
    operands = [blocks.reshape(slots, channels, voxels), conv_weight, neighbours.reshape(slots, 26), table, conv_bias[None], head_bias[None]]
    acc, pool, wf, meta, bias = pl.pallas_call(
        functools.partial(exchange_kernel, sizes, slots),
        out_shape=[
            jax.ShapeDtypeStruct((slots, 16, cout, 256), F32),
            jax.ShapeDtypeStruct(((ZERO + 1) * slots, channels, 256), blocks.dtype),
            jax.ShapeDtypeStruct((6, 3 * cout, 3 * channels), BF16),
            jax.ShapeDtypeStruct((4 * slots, 128), jnp.int32),
            jax.ShapeDtypeStruct((2, cout, 128), F32),
        ],
        in_specs=[hbm] * 6,
        out_specs=[vmem] * 5,
        scratch_shapes=[
            pltpu.VMEM((slots, channels, voxels), BF16),
            pltpu.VMEM((slots, 18, 3 * channels, 256), BF16),
            pltpu.VMEM((3 * cout, 9 * channels), BF16),
            pltpu.VMEM(conv_weight.shape, BF16),
            pltpu.VMEM((slots, 26), jnp.int32),
            pltpu.VMEM(table.shape, jnp.int32),
            pltpu.VMEM((2, cout), F32),
            pltpu.VMEM((27, channels // 3, 128), BF16),
            pltpu.VMEM((27, channels // 3, 128), BF16),
            pltpu.SemaphoreType.DMA((slots, 2)),
            pltpu.SemaphoreType.DMA((5,)),
            pltpu.SemaphoreType.DMA((27,)),
            pltpu.SemaphoreType.DMA((27,)),
        ],
        compiler_params=pltpu.CompilerParams(collective_id=0, has_side_effects=True, vmem_limit_bytes=24 << 20),
        name="exchange",
    )(*[pltpu.with_memory_space_constraint(operand, pltpu.HBM) for operand in operands])
    out = finish(slots, voxels, meta, block_count, acc, pool, wf, bias, head_weight)
    return out.reshape(1, 1, slots, cout, voxels)


def solution(mesh):
    placed = (
        P("gx", "gz", "gy", None, None),
        P("gx", "gz", "gy"),
        P("gx", "gz", "gy", None),
        P(),
        P(),
        P(),
        P(),
    )
    return jax.shard_map(
        functools.partial(body, dict(mesh.shape)),
        mesh=mesh,
        in_specs=placed,
        out_specs=P("gx", "gz", "gy", None, None),
        check_vma=False,
    )
```

```python
import functools

import jax
import jax.numpy as jnp
import numpy as np
from jax import lax
from jax.experimental import pallas as pl
from jax.experimental.pallas import tpu as pltpu
from jax.sharding import PartitionSpec as P

AXES = ("gx", "gy", "gz")
OFFSETS = [(a, b, c) for a in (-1, 0, 1) for b in (-1, 0, 1) for c in (-1, 0, 1)]
LINKS = [o for o in OFFSETS if o != (0, 0, 0)]
F32 = jnp.float32
BF16 = jnp.bfloat16
MESH = pl.DeviceIdType.MESH


def weight(d):
    return sum(map(abs, d))


def last(step):
    return 0 if step == -1 else 1


def far(step):
    return 15 if step == -1 else 0


KINDS = {("own", a, s): 2 * a + s for a in range(3) for s in (0, 1)}
KINDS |= {("came", a, s): 6 + 2 * a + s for a in range(3) for s in (0, 1)}
for _d in LINKS:
    if weight(_d) > 1:
        KINDS[_d] = len(KINDS)
ZERO = len(KINDS)


def entry_of(d):
    if weight(d) > 1:
        return KINDS[d]
    axis = [i for i in range(3) if d[i]][0]
    return KINDS["came", axis, last(d[axis])]


def piece_of(o, c):
    e = tuple(o[a] if c >> a & 1 else 0 for a in range(3))
    if c:
        kind = entry_of(e)
    else:
        axis = [a for a in range(3) if o[a]][0]
        kind = KINDS["own", axis, last(o[axis])]
    x, y, z = (far(step) if step else 0 for step in o)
    if c == 7:
        lane = 0
    elif c == 3:
        lane = z
    elif c in (4, 5):
        lane = y * 16 + x
    elif c in (2, 6) or not o[0]:
        lane = x * 16 + z
    else:
        lane = y * 16 + z
    return kind, lane


PARTS = 9
FACE, SIDE, RING = 0, 1, 2


def face_parts(axis, step):
    def off(**steps):
        return tuple(steps.get(name, 0) for name in "xyz")

    name = "xyz"[axis]
    parts = [(off(**{name: step}), {0: (0, 1), 1: (0, 2), 2: (0, 4)}[axis])]
    for e in (-1, 1):
        parts.append((off(**{name: step, "x" if axis == 2 else "z": e}), {0: (0, 1), 1: (0, 2, 6), 2: (4, 5)}[axis]))
    for r in (-1, 1):
        if axis == 1:
            parts.append((off(y=step), ()))
        else:
            parts.append((off(**{name: step, "y": r}), {0: (0, 1, 2, 3), 2: (4,)}[axis]))
    for e in (-1, 1):
        for r in (-1, 1):
            parts.append((off(x=step, y=r, z=e), tuple(range(8))) if axis == 0 else (off(**{name: step}), ()))
    return parts


def plan(slots):
    entry = np.full((8, 128), -1, np.int32)
    lane = np.zeros((8, 128), np.int32)
    pick = np.zeros((32, 128), np.int32)
    needs = np.zeros((128, 128), np.int32)
    for f in range(6):
        for k, (o, codes) in enumerate(face_parts(f // 2, (-1, 1)[f % 2])):
            j = f * PARTS + k
            pick[LINKS.index(o), j] = 1
            for c in codes:
                if any(c >> a & 1 and o[a] == 0 for a in range(3)):
                    continue
                kind, at = piece_of(o, c)
                entry[c, j], lane[c, j] = kind * slots, at
            needs[j, FACE] = 1
            needs[j, SIDE] = f >= 2
            needs[j, RING + f // 2] = k >= 3
    return np.concatenate([entry, lane, pick, needs])


def roll(value, shift):
    shift %= 128
    return pltpu.roll(value, shift, 1) if shift else value


def rows_of(y, cout):
    lane = lax.broadcasted_iota(jnp.int32, (cout, 128), 1)
    first, final = lane < 16, lane >= 112
    down = [roll(y[0:cout, at : at + 128], 16) for at in (0, 128)]
    up = [roll(y[2 * cout :, at : at + 128], -16) for at in (0, 128)]
    zero = jnp.zeros_like(down[0])
    low = y[cout : 2 * cout, 0:128] + jnp.where(first, zero, down[0]) + jnp.where(final, up[1], up[0])
    high = y[cout : 2 * cout, 128:256] + jnp.where(first, down[0], down[1]) + jnp.where(final, zero, up[1])
    return low, high


def exchange_kernel(
    sizes, row, slots, blk_hbm, cw_hbm, links_hbm, plan_hbm, cb_hbm, hb_hbm, acc, pool, wf, meta, bias,
    blk, planes, w, cw, links, table, biases, gone, came, passed, load_sem, aux_sem, send_sem, recv_sem, half_send, half_recv, pass_send, pass_recv,
):
    channels = blk.shape[1]
    cout = w.shape[0] // 3
    here = {axis: lax.axis_index(axis) for axis in AXES}

    def exists(d):
        ok = None
        for axis, step in zip(AXES, d):
            if step:
                at = here[axis] + step
                good = jnp.logical_and(at >= 0, at < sizes[axis])
                ok = good if ok is None else jnp.logical_and(ok, good)
        return ok

    def target(d):
        return {axis: here[axis] + step for axis, step in zip(AXES, d) if step}

    def turn(at, step):
        if not row:
            return at < 0
        inside = jnp.logical_and(at + step >= 0, at + step < sizes["gx"])
        return jnp.logical_and(inside, lax.rem(at + row, row) == (row - 1 if step == 1 else 0))

    def via(at, step):
        return at + step * (row)

    def relays(at, step):
        origin = at - step * (row)
        known = jnp.logical_and(origin >= 0, origin < sizes["gx"])
        return jnp.logical_and(known, turn(origin, step))

    def halves(step, slot):
        x = 15 if step == 1 else 0
        side = last(-step)
        src = blk_hbm.at[slot, :, x * 256 : x * 256 + 256]
        into = KINDS["came", 0, side] * slots + slot
        sems = dict(send_sem=half_send.at[side, slot], device_id_type=MESH)
        direct = pltpu.make_async_remote_copy(
            src_ref=src, dst_ref=pool.at[into], recv_sem=half_recv.at[side, slot],
            device_id={"gx": here["gx"] + step}, **sems,
        )
        around = pltpu.make_async_remote_copy(
            src_ref=src, dst_ref=passed.at[side], recv_sem=pass_recv.at[side],
            device_id={"gx": via(here["gx"], step)}, **sems,
        )
        return direct, around

    def pass_on(step):
        side = last(-step)
        into = KINDS["came", 0, side] * slots + slots - 1
        return pltpu.make_async_remote_copy(
            src_ref=passed.at[side], dst_ref=pool.at[into], send_sem=pass_send.at[side],
            recv_sem=half_recv.at[side, slots - 1],
            device_id={"gx": here["gx"] - step * ((row) - 1)}, device_id_type=MESH,
        )

    def turns(step):
        return turn(here["gx"], step)

    partners = [d for d in LINKS if not d[1] or weight(d) == 1]
    messages = [d for d in LINKS if weight(d) < 3]
    span = blk.shape[2] // 2
    loads = [
        pltpu.make_async_copy(
            blk_hbm.at[u, :, k * span : k * span + span], blk.at[u, :, k * span : k * span + span], load_sem.at[u, k]
        )
        for u in range(slots)
        for k in (0, 1)
    ]
    others = [
        pltpu.make_async_copy(src, dst, aux_sem.at[i])
        for i, (src, dst) in enumerate([(cw_hbm, cw), (links_hbm, links), (plan_hbm, table), (cb_hbm, biases.at[0:1]), (hb_hbm, biases.at[1:2])])
    ]
    for other in others:
        other.start()
    for load in loads:
        load.start()
    barrier = pltpu.get_barrier_semaphore()
    for d in partners:
        @pl.when(exists(d))
        def _():
            pl.semaphore_signal(barrier, inc=1, device_id=target(d), device_id_type=MESH)
    def greet(when, device):
        @pl.when(when)
        def _():
            pl.semaphore_signal(barrier, inc=1, device_id={"gx": device}, device_id_type=MESH)

    extra = 0
    for step in (-1, 1):
        origin = here["gx"] - step * (row)
        greet(relays(here["gx"], step), origin)
        extra = extra + jnp.where(turns(step), 1, 0)
        if row > 2:
            greet(turn(here["gx"] - step, step), via(here["gx"] - step, step))
            extra = extra + jnp.where(relays(here["gx"], step), 1, 0)
    near = {
        axis: jnp.where(here[axis] > 0, 1, 0) + jnp.where(here[axis] < sizes[axis] - 1, 1, 0) for axis in AXES
    }

    def own(axis, side, u):
        return KINDS["own", axis, side] * slots + u

    def copy_of(d):
        to = d if weight(d) == 1 else (d[0], 0, d[2])
        e = (-to[0], d[1] if weight(d) > 1 else -d[1], -to[2])
        if weight(d) > 1:
            src, dst = gone.at[OFFSETS.index(d)], came.at[OFFSETS.index(e)]
        else:
            axis = [i for i in range(3) if d[i]][0]
            into = entry_of(e) * slots
            dst = pool.at[into : into + slots]
            kept = own(axis, last(-d[axis]), 0)
            src = pool.at[kept : kept + slots]
        return pltpu.make_async_remote_copy(
            src_ref=src,
            dst_ref=dst,
            send_sem=send_sem.at[OFFSETS.index(d)],
            recv_sem=recv_sem.at[OFFSETS.index(e)],
            device_id=target(to),
            device_id_type=MESH,
        )

    def start(d):
        @pl.when(exists(d))
        def _():
            copy_of(d).start()

    def sender(e):
        return (-e[0], e[1] if weight(e) > 1 else -e[1], -e[2])

    for u in range(slots):
        pool[ZERO * slots + u] = jnp.zeros(pool.shape[1:], pool.dtype)
        for end in (0, 17):
            planes[u, end] = jnp.zeros(planes.shape[2:], planes.dtype)
    others[0].wait()
    depth = 3 * channels
    for a in range(3):
        for b in range(3):
            at = (a * 9 + b * 3) * channels
            taps = cw[:, at : at + depth]
            w[b * cout : (b + 1) * cout, a * depth : (a + 1) * depth] = taps
            if a != 1:
                wf[last(a - 1), b * cout : (b + 1) * cout, :] = taps
            if b != 1:
                wf[2 + last(b - 1), a * cout : (a + 1) * cout, :] = taps
            for k in (0, 2):
                wf[4 + k // 2, b * cout : (b + 1) * cout, a * channels : (a + 1) * channels] = taps[
                    :, k * channels : (k + 1) * channels
                ]

    for other in others[1:]:
        other.wait()
    value = jnp.dot(links[...].astype(F32), table[16 : 16 + links.shape[1], :].astype(F32), preferred_element_type=F32)
    value = value.astype(jnp.int32)
    code, slot = value >> 1, value & 1
    entry, lies = jnp.full_like(value, -1), jnp.zeros_like(value)
    for c in range(8):
        entry = jnp.where(code == c, table[c : c + 1, :], entry)
        lies = jnp.where(code == c, table[8 + c : 9 + c, :], lies)
    needed = jnp.dot(
        jnp.where(entry >= 0, 1.0, 0.0), table[48:176, :].astype(F32), preferred_element_type=F32
    ).astype(jnp.int32)
    meta[0:slots, :] = jnp.where(entry >= 0, entry + slot, ZERO * slots)
    meta[slots : 2 * slots, :] = lies
    meta[2 * slots : 3 * slots, :] = needed
    eye = lax.broadcasted_iota(jnp.int32, (cout, cout), 0) == lax.broadcasted_iota(jnp.int32, (cout, cout), 1)
    for i in (0, 1):
        column = jnp.sum(jnp.where(eye, biases[i : i + 1, :], 0.0), axis=1, keepdims=True)
        bias[i] = jnp.zeros(bias.shape[1:], F32) + column

    for load in loads:
        load.wait()

    lane = lax.broadcasted_iota(jnp.int32, (channels, 128), 1)
    group, place = lane // 16, lane % 16
    third = channels // 3
    cut = lax.broadcasted_iota(jnp.int32, (third, 128), 1)
    cut_group, cut_place = cut // 16, cut % 16

    def tile(u, x, half):
        at = x * 256 + half * 128
        return blk[u, :, at : at + 128]

    def third_of(entry, part, half):
        return pool[entry, part * third : part * third + third, half * 128 : half * 128 + 128]

    for u in range(slots):
        for half in (0, 1):
            before, after = None, None
            for k in range(8):
                x = half * 8 + k
                moved = roll(jnp.where(group == 7, tile(u, x, 1), tile(u, x, 0)), k * 16)
                after = moved if after is None else jnp.where(group == k, moved, after)
                before = moved if before is None else jnp.where(group == (k + 7) % 8, moved, before)
            lanes = slice(half * 128, half * 128 + 128)
            pool[own(1, 0, u), :, lanes] = roll(before, 16)
            pool[own(1, 1, u), :, lanes] = after
    pl.semaphore_wait(barrier, (1 + near["gx"]) * (1 + near["gz"]) - 1 + near["gy"] + extra)
    for slot in range(slots)[::-1]:
        for step in (1, -1):
            @pl.when(exists((step, 0, 0)))
            def _():
                direct, around = halves(step, slot)
                if slot < slots - 1:
                    direct.start()
                    return
                pl.when(turns(step))(around.start)
                pl.when(jnp.logical_not(turns(step)))(direct.start)
    start((0, 1, 0))
    start((0, -1, 0))
    for u in range(slots):
        for half in (0, 1):
            before, after = None, None
            for x in range(16):
                moved = roll(tile(u, x, half), x)
                after = moved if after is None else jnp.where(place == x, moved, after)
                before = moved if before is None else jnp.where(place == (x + 15) % 16, moved, before)
            lanes = slice(half * 128, half * 128 + 128)
            pool[own(2, 0, u), :, lanes] = roll(before, -15)
            pool[own(2, 1, u), :, lanes] = after
    start((0, 0, 1))
    start((0, 0, -1))
    for u in range(slots):
        pool[own(0, 0, u)] = blk[u, :, 15 * 256 : 16 * 256]
        pool[own(0, 1, u)] = blk[u, :, 0:256]

    def strips(d, entry, col):
        made = None
        for part in range(3):
            for u in range(slots):
                for half in (0, 1):
                    goes = (part * slots + u) * 2 + half
                    moved = roll(third_of(entry(u), part, half), goes - col)
                    made = moved if made is None else jnp.where(cut_place == goes, moved, made)
        return made

    def corner_lane(dy, u, part):
        return part * 16 + 12 + last(dy) * slots + u

    for dy in (-1, 1):
        @pl.when(exists((0, dy, 0)))
        def _():
            copy_of((0, -dy, 0)).wait_recv()
    for dy in (-1, 1):
        @pl.when(exists((0, dy, 0)))
        def _():
            def entry(u):
                return KINDS["came", 1, last(dy)] * slots + u

            for dx in (1, -1):
                made = None
                for part in range(3):
                    for u in range(slots):
                        goes = part * slots + u
                        half = 1 if dx == 1 else 0
                        moved = roll(third_of(entry(u), part, half), (goes - 7 * half) * 16)
                        made = moved if made is None else jnp.where(cut_group == goes, moved, made)
                gone[OFFSETS.index((dx, dy, 0))] = made
                start((dx, dy, 0))
            for dz in (1, -1):
                gone[OFFSETS.index((0, dy, dz))] = strips((0, dy, dz), entry, 15 if dz == 1 else 0)
                start((0, dy, dz))
    for dx in (1, -1):
        for dz in (1, -1):
            x, z = (15 if dx == 1 else 0), (15 if dz == 1 else 0)
            made = strips((dx, 0, dz), lambda u: own(2, last(-dz), u), x)
            for dy in (-1, 1):
                for u in range(slots):
                    for part in range(3):
                        goes = corner_lane(dy, u, part)
                        half = x // 8
                        moved = roll(
                            third_of(KINDS["came", 1, last(dy)] * slots + u, part, half), goes - (x * 16 + z) % 128
                        )
                        made = jnp.where(cut == goes, moved, made)
            gone[OFFSETS.index((dx, 0, dz))] = made
            start((dx, 0, dz))

    def build(u, p):
        for half in (0, 1):
            lanes = slice(128 * half, 128 * half + 128)
            value = blk[u, :, (p - 1) * 256 + 128 * half : (p - 1) * 256 + 128 * half + 128]
            planes[u, p, channels : 2 * channels, lanes] = value
            for dz in (-1, 1):
                moved = jnp.where(place == (0 if dz == -1 else 15), jnp.zeros_like(value), roll(value, -dz))
                planes[u, p, (dz + 1) * channels : (dz + 2) * channels, lanes] = moved

    def per_slot(u, _):
        build(u, 1)
        for x in range(16):
            if x < 15:
                build(u, x + 2)
            y = jnp.dot(w[...], planes[u, x : x + 3].reshape(3 * depth, 256), preferred_element_type=F32)
            acc[u, x, :, 0:128], acc[u, x, :, 128:256] = rows_of(y, cout)
        return 0

    per_slot(0, 0)
    for step in (1, -1):
        @pl.when(relays(here["gx"], step))
        def _():
            halves(step, slots - 1)[1].wait_recv()
            pass_on(step).start()

    for u in range(1, slots):
        per_slot(u, 0)

    for e in sorted(messages, key=lambda e: -weight(e)):
        @pl.when(exists(e))
        def _():
            if weight(e) == 1 and e[0]:
                for slot in range(slots):
                    halves(-e[0], slot)[0].wait_recv()
            elif weight(e) > 1 or not e[1]:
                copy_of(sender(e)).wait_recv()
            if weight(e) == 1:
                return
            got = came[OFFSETS.index(e)]
            for u in range(slots):
                for part in range(3):
                    rows = slice(part * third, part * third + third)
                    if not e[2]:
                        pool[KINDS[e] * slots + u, rows, 0:128] = roll(got, -16 * (part * slots + u))
                        continue
                    for half in (0, 1):
                        lies = (part * slots + u) * 2 + half
                        col = far(e[2] if e[1] else e[0])
                        pool[KINDS[e] * slots + u, rows, half * 128 : half * 128 + 128] = roll(got, col - lies)
                    if not e[1]:
                        for dy in (-1, 1):
                            pool[KINDS[e[0], dy, e[2]] * slots + u, rows, 0:128] = roll(got, -corner_lane(dy, u, part))
    for d in messages:
        @pl.when(exists(d))
        def _():
            if weight(d) > 1 or not d[0]:
                copy_of(d).wait_send()
            else:
                for slot in range(slots):
                    halves(d[0], slot)[0].wait_send()
    for step in (1, -1):
        pl.when(relays(here["gx"], step))(lambda: pass_on(step).wait_send())


def finish_kernel(slots, meta, count, acc, pool, wf, bias, hw, out, stack, ring, faces, made, out_sem):
    channels = pool.shape[1]
    cout = hw.shape[0]
    lane = lax.broadcasted_iota(jnp.int32, (channels, 128), 1)
    group, place = lane // 16, lane % 16
    lane_out = lax.broadcasted_iota(jnp.int32, (cout, 128), 1)
    group_out, place_out = lane_out // 16, lane_out % 16
    at_ends = jnp.logical_or(place_out == 0, place_out == 15)
    row_bias, head_bias = bias[0], bias[1]
    both_head = jnp.concatenate([head_bias, head_bias], 1)

    def entry(s, f, k):
        return meta[s, f * PARTS + k]

    def fetch(s, f, k, goes):
        lies = meta[slots + s, f * PARTS + k]
        got = pool[entry(s, f, k), :, pl.ds(pl.multiple_of((lies // 128) * 128, 128), 128)]
        return pltpu.roll(got, lax.rem(goes - lies + 256, 128), 1)

    def face(s, f):
        for half in (0, 1):
            lanes = slice(half * 128, half * 128 + 128)
            value = pool[entry(s, f, 0), :, lanes]
            stack[f, channels : 2 * channels, lanes] = value
            for e in (-1, 1):
                at = 0 if e == -1 else 15
                piece = roll(pool[entry(s, f, 1 + last(e)), :, lanes], 15 * e)
                stack[f, (e + 1) * channels : (e + 2) * channels, lanes] = jnp.where(
                    place == at, piece, roll(value, -e)
                )
        y = jnp.dot(wf[f], stack[f], preferred_element_type=F32)
        faces[f, :, 0:128], faces[f, :, 128:256] = rows_of(y, cout)

    def rings(s, axis):
        line = None
        for i in (0, 1):
            for r in (0, 1):
                goes = 1 - i if r else 6 + i
                got = fetch(s, 2 * axis + i, 3 + r, goes * 16)
                line = got if line is None else jnp.where(group == goes, got, line)
        ring[channels : 2 * channels, :] = line
        for e in (-1, 1):
            at = 0 if e == -1 else 15
            moved = jnp.where(place == at, jnp.zeros_like(line), roll(line, -e))
            if axis == 0:
                for i in (0, 1):
                    for r in (0, 1):
                        goes = (1 - i if r else 6 + i) * 16 + at
                        moved = jnp.where(lane == goes, fetch(s, i, 5 + 2 * last(e) + r, goes), moved)
            ring[(e + 1) * channels : (e + 2) * channels, :] = moved
        for i in (0, 1):
            f = 2 * axis + i
            y = jnp.dot(wf[f], ring[...], preferred_element_type=F32)
            faces[f, :, 0:128] += jnp.where(group_out == 0, roll(y[0:cout], 32 - 16 * i), 0.0)
            faces[f, :, 128:256] += jnp.where(group_out == 7, roll(y[2 * cout :], -32 + 16 * i), 0.0)

    def plane(s, x, keep, with_faces, with_sides):
        hidden = []
        for half in (0, 1):
            lanes = slice(half * 128, half * 128 + 128)
            v = acc[s, x, :, lanes] + row_bias
            if with_faces and x in (0, 15):
                v = v + faces[x // 15, :, lanes]
            if with_sides:
                goes = 7 if half else 0
                strip = faces[2 + half, :, (x // 8) * 128 : (x // 8) * 128 + 128]
                v = v + jnp.where(group_out == goes, roll(strip, (goes - x % 8) * 16), 0.0)
                ends = jnp.where(place_out == x, faces[4, :, lanes], faces[5, :, lanes])
                v = v + jnp.where(at_ends, roll(ends, -x), 0.0)
            hidden.append(jnp.maximum(v, 0.0).astype(BF16))
        mixed = jnp.dot(hw[...], jnp.concatenate(hidden, 1), preferred_element_type=F32) + both_head
        made[s, :, x * 256 : x * 256 + 256] = (mixed * keep).astype(made.dtype)

    def chunk(s, q):
        lanes = pl.ds(q * 1024, 1024)
        return pltpu.make_async_copy(made.at[s, :, lanes], out.at[s, :, lanes], out_sem.at[s, q])

    def per_slot(s, _):
        keep = jnp.where(s < count[0, 0, 0], 1.0, 0.0)
        any_face = meta[2 * slots + s, FACE] > 0
        any_side = meta[2 * slots + s, SIDE] > 0

        @pl.when(any_face)
        def _():
            for f in range(6):
                face(s, f)
            for axis in (0, 2):
                pl.when(meta[2 * slots + s, RING + axis] > 0)(functools.partial(rings, s, axis))

        def run(with_faces, with_sides):
            if with_sides:
                for half in (0, 1):
                    lanes = slice(half * 128, half * 128 + 128)
                    faces[5, :, lanes] = roll(faces[5, :, lanes], 15)
            for q in range(4):
                for k in range(4):
                    plane(s, q * 4 + k, keep, with_faces, with_sides)
                chunk(s, q).start()

        pl.when(any_side)(lambda: run(True, True))
        pl.when(jnp.logical_and(any_face, jnp.logical_not(any_side)))(lambda: run(True, False))
        pl.when(jnp.logical_not(any_face))(lambda: run(False, False))
        return 0

    lax.fori_loop(0, slots, per_slot, 0)
    for s in range(slots):
        for q in range(4):
            chunk(s, q).wait()


def finish(slots, voxels, meta, block_count, acc, pool, wf, bias, head_weight):
    channels = pool.shape[1]
    cout = head_weight.shape[0]
    return pl.pallas_call(
        functools.partial(finish_kernel, slots),
        out_shape=jax.ShapeDtypeStruct((slots, cout, voxels), BF16),
        in_specs=[pl.BlockSpec(memory_space=pltpu.SMEM)] * 2 + [pl.BlockSpec(memory_space=pltpu.VMEM)] * 5,
        out_specs=pl.BlockSpec(memory_space=pltpu.HBM),
        scratch_shapes=[
            pltpu.VMEM((6, 3 * channels, 256), BF16),
            pltpu.VMEM((3 * channels, 128), BF16),
            pltpu.VMEM((6, cout, 256), F32),
            pltpu.VMEM((slots, cout, voxels), BF16),
            pltpu.SemaphoreType.DMA((slots, 4)),
        ],
        compiler_params=pltpu.CompilerParams(vmem_limit_bytes=20 << 20),
        name="finish",
    )(meta, block_count, acc, pool, wf, bias, head_weight)


def body(sizes, row, blocks, block_count, neighbours, conv_weight, conv_bias, head_weight, head_bias):
    slots, channels, voxels = blocks.shape[2:]
    cout = head_weight.shape[0]
    vmem = pl.BlockSpec(memory_space=pltpu.VMEM)
    hbm = pl.BlockSpec(memory_space=pltpu.HBM)
    table = jnp.asarray(plan(slots))
    operands = [blocks.reshape(slots, channels, voxels), conv_weight, neighbours.reshape(slots, 26), table, conv_bias[None], head_bias[None]]
    acc, pool, wf, meta, bias = pl.pallas_call(
        functools.partial(exchange_kernel, sizes, row, slots),
        out_shape=[
            jax.ShapeDtypeStruct((slots, 16, cout, 256), F32),
            jax.ShapeDtypeStruct(((ZERO + 1) * slots, channels, 256), blocks.dtype),
            jax.ShapeDtypeStruct((6, 3 * cout, 3 * channels), BF16),
            jax.ShapeDtypeStruct((4 * slots, 128), jnp.int32),
            jax.ShapeDtypeStruct((2, cout, 128), F32),
        ],
        in_specs=[hbm] * 6,
        out_specs=[vmem] * 5,
        scratch_shapes=[
            pltpu.VMEM((slots, channels, voxels), BF16),
            pltpu.VMEM((slots, 18, 3 * channels, 256), BF16),
            pltpu.VMEM((3 * cout, 9 * channels), BF16),
            pltpu.VMEM(conv_weight.shape, BF16),
            pltpu.VMEM((slots, 26), jnp.int32),
            pltpu.VMEM(table.shape, jnp.int32),
            pltpu.VMEM((2, cout), F32),
            pltpu.VMEM((27, channels // 3, 128), BF16),
            pltpu.VMEM((27, channels // 3, 128), BF16),
            pltpu.VMEM((2, channels, 256), BF16),
            pltpu.SemaphoreType.DMA((slots, 2)),
            pltpu.SemaphoreType.DMA((5,)),
            pltpu.SemaphoreType.DMA((27,)),
            pltpu.SemaphoreType.DMA((27,)),
            pltpu.SemaphoreType.DMA((2, slots)),
            pltpu.SemaphoreType.DMA((2, slots)),
            pltpu.SemaphoreType.DMA((2,)),
            pltpu.SemaphoreType.DMA((2,)),
        ],
        compiler_params=pltpu.CompilerParams(collective_id=0, has_side_effects=True, vmem_limit_bytes=24 << 20),
        name="exchange",
    )(*[pltpu.with_memory_space_constraint(operand, pltpu.HBM) for operand in operands])
    out = finish(slots, voxels, meta, block_count, acc, pool, wf, bias, head_weight)
    return out.reshape(1, 1, slots, cout, voxels)


def row_length(mesh):
    axis = mesh.axis_names.index("gx")
    line = np.moveaxis(mesh.devices, axis, 0).reshape(mesh.shape["gx"], -1)[:, 0]
    coords = [np.asarray(device.coords) for device in line]
    for i in range(1, len(coords)):
        if np.count_nonzero(coords[i] != coords[i - 1]) > 1:
            return i
    return 0


def solution(mesh):
    placed = (
        P("gx", "gz", "gy", None, None),
        P("gx", "gz", "gy"),
        P("gx", "gz", "gy", None),
        P(),
        P(),
        P(),
        P(),
    )
    return jax.shard_map(
        functools.partial(body, dict(mesh.shape), row_length(mesh)),
        mesh=mesh,
        in_specs=placed,
        out_specs=P("gx", "gz", "gy", None, None),
        check_vma=False,
    )
```

```python
import functools

import jax
import jax.numpy as jnp
import numpy as np
from jax import lax
from jax.experimental import pallas as pl
from jax.experimental.pallas import tpu as pltpu
from jax.sharding import PartitionSpec as P

AXES = ("gx", "gy", "gz")
OFFSETS = [(a, b, c) for a in (-1, 0, 1) for b in (-1, 0, 1) for c in (-1, 0, 1)]
LINKS = [o for o in OFFSETS if o != (0, 0, 0)]
F32 = jnp.float32
BF16 = jnp.bfloat16
MESH = pl.DeviceIdType.MESH


def weight(d):
    return sum(map(abs, d))


def last(step):
    return 0 if step == -1 else 1


def far(step):
    return 15 if step == -1 else 0


KINDS = {("own", a, s): 2 * a + s for a in range(3) for s in (0, 1)}
KINDS |= {("came", a, s): 6 + 2 * a + s for a in range(3) for s in (0, 1)}
for _d in LINKS:
    if weight(_d) > 1:
        KINDS[_d] = len(KINDS)
ZERO = len(KINDS)


def entry_of(d):
    if weight(d) > 1:
        return KINDS[d]
    axis = [i for i in range(3) if d[i]][0]
    return KINDS["came", axis, last(d[axis])]


def piece_of(o, c):
    e = tuple(o[a] if c >> a & 1 else 0 for a in range(3))
    if c:
        kind = entry_of(e)
    else:
        axis = [a for a in range(3) if o[a]][0]
        kind = KINDS["own", axis, last(o[axis])]
    x, y, z = (far(step) if step else 0 for step in o)
    if c == 7:
        lane = 0
    elif c == 3:
        lane = z
    elif c in (4, 5):
        lane = y * 16 + x
    elif c in (2, 6) or not o[0]:
        lane = x * 16 + z
    else:
        lane = y * 16 + z
    return kind, lane


PARTS = 9
FACE, SIDE_Y, SIDE_Z, RING = 0, 1, 2, 3


def face_parts(axis, step):
    def off(**steps):
        return tuple(steps.get(name, 0) for name in "xyz")

    name = "xyz"[axis]
    parts = [(off(**{name: step}), {0: (0, 1), 1: (0, 2), 2: (0, 4)}[axis])]
    for e in (-1, 1):
        parts.append((off(**{name: step, "x" if axis == 2 else "z": e}), {0: (0, 1), 1: (0, 2, 6), 2: (4, 5)}[axis]))
    for r in (-1, 1):
        if axis == 1:
            parts.append((off(y=step), ()))
        else:
            parts.append((off(**{name: step, "y": r}), {0: (0, 1, 2, 3), 2: (4,)}[axis]))
    for e in (-1, 1):
        for r in (-1, 1):
            parts.append((off(x=step, y=r, z=e), tuple(range(8))) if axis == 0 else (off(**{name: step}), ()))
    return parts


def plan(slots):
    entry = np.full((8, 128), -1, np.int32)
    lane = np.zeros((8, 128), np.int32)
    pick = np.zeros((32, 128), np.int32)
    needs = np.zeros((128, 128), np.int32)
    for f in range(6):
        for k, (o, codes) in enumerate(face_parts(f // 2, (-1, 1)[f % 2])):
            j = f * PARTS + k
            pick[LINKS.index(o), j] = 1
            for c in codes:
                if any(c >> a & 1 and o[a] == 0 for a in range(3)):
                    continue
                kind, at = piece_of(o, c)
                entry[c, j], lane[c, j] = kind * slots, at
            needs[j, FACE] = 1
            needs[j, SIDE_Y] = f in (2, 3)
            needs[j, SIDE_Z] = f in (4, 5)
            needs[j, RING + f // 2] = k >= 3
    return np.concatenate([entry, lane, pick, needs])


def roll(value, shift):
    shift %= 128
    return pltpu.roll(value, shift, 1) if shift else value


def rows_of(y, cout):
    lane = lax.broadcasted_iota(jnp.int32, (cout, 128), 1)
    first, final = lane < 16, lane >= 112
    down = [roll(y[0:cout, at : at + 128], 16) for at in (0, 128)]
    up = [roll(y[2 * cout :, at : at + 128], -16) for at in (0, 128)]
    zero = jnp.zeros_like(down[0])
    low = y[cout : 2 * cout, 0:128] + jnp.where(first, zero, down[0]) + jnp.where(final, up[1], up[0])
    high = y[cout : 2 * cout, 128:256] + jnp.where(first, down[0], down[1]) + jnp.where(final, zero, up[1])
    return low, high


def exchange_kernel(
    sizes, row, slots, blk_hbm, cw_hbm, links_hbm, plan_hbm, cb_hbm, hb_hbm, acc, pool, wf, meta, bias,
    blk, planes, w, cw, links, table, biases, gone, came, passed, load_sem, aux_sem, send_sem, recv_sem, half_send, half_recv, pass_send, pass_recv,
):
    channels = blk.shape[1]
    cout = w.shape[0] // 3
    here = {axis: lax.axis_index(axis) for axis in AXES}

    def exists(d):
        ok = None
        for axis, step in zip(AXES, d):
            if step:
                at = here[axis] + step
                good = jnp.logical_and(at >= 0, at < sizes[axis])
                ok = good if ok is None else jnp.logical_and(ok, good)
        return ok

    def target(d):
        return {axis: here[axis] + step for axis, step in zip(AXES, d) if step}

    def turn(at, step):
        if not row:
            return at < 0
        inside = jnp.logical_and(at + step >= 0, at + step < sizes["gx"])
        return jnp.logical_and(inside, lax.rem(at + row, row) == (row - 1 if step == 1 else 0))

    def via(at, step):
        return at + step * (row)

    def relays(at, step):
        origin = at - step * (row)
        known = jnp.logical_and(origin >= 0, origin < sizes["gx"])
        return jnp.logical_and(known, turn(origin, step))

    def halves(step, slot):
        x = 15 if step == 1 else 0
        side = last(-step)
        src = blk_hbm.at[slot, :, x * 256 : x * 256 + 256]
        into = KINDS["came", 0, side] * slots + slot
        sems = dict(send_sem=half_send.at[side, slot], device_id_type=MESH)
        direct = pltpu.make_async_remote_copy(
            src_ref=src, dst_ref=pool.at[into], recv_sem=half_recv.at[side, slot],
            device_id={"gx": here["gx"] + step}, **sems,
        )
        around = pltpu.make_async_remote_copy(
            src_ref=src, dst_ref=passed.at[side], recv_sem=pass_recv.at[side],
            device_id={"gx": via(here["gx"], step)}, **sems,
        )
        return direct, around

    def pass_on(step):
        side = last(-step)
        into = KINDS["came", 0, side] * slots + slots - 1
        return pltpu.make_async_remote_copy(
            src_ref=passed.at[side], dst_ref=pool.at[into], send_sem=pass_send.at[side],
            recv_sem=half_recv.at[side, slots - 1],
            device_id={"gx": here["gx"] - step * ((row) - 1)}, device_id_type=MESH,
        )

    def turns(step):
        return turn(here["gx"], step)

    partners = [d for d in LINKS if not d[1] or weight(d) == 1]
    messages = [d for d in LINKS if weight(d) < 3]
    span = blk.shape[2] // 2
    loads = [
        pltpu.make_async_copy(
            blk_hbm.at[u, :, k * span : k * span + span], blk.at[u, :, k * span : k * span + span], load_sem.at[u, k]
        )
        for u in range(slots)
        for k in (0, 1)
    ]
    others = [
        pltpu.make_async_copy(src, dst, aux_sem.at[i])
        for i, (src, dst) in enumerate([(cw_hbm, cw), (links_hbm, links), (plan_hbm, table), (cb_hbm, biases.at[0:1]), (hb_hbm, biases.at[1:2])])
    ]
    for other in others:
        other.start()
    for load in loads:
        load.start()
    barrier = pltpu.get_barrier_semaphore()
    for d in partners:
        @pl.when(exists(d))
        def _():
            pl.semaphore_signal(barrier, inc=1, device_id=target(d), device_id_type=MESH)
    def greet(when, device):
        @pl.when(when)
        def _():
            pl.semaphore_signal(barrier, inc=1, device_id={"gx": device}, device_id_type=MESH)

    extra = 0
    for step in (-1, 1):
        origin = here["gx"] - step * (row)
        greet(relays(here["gx"], step), origin)
        extra = extra + jnp.where(turns(step), 1, 0)
        if row > 2:
            greet(turn(here["gx"] - step, step), via(here["gx"] - step, step))
            extra = extra + jnp.where(relays(here["gx"], step), 1, 0)
    near = {
        axis: jnp.where(here[axis] > 0, 1, 0) + jnp.where(here[axis] < sizes[axis] - 1, 1, 0) for axis in AXES
    }

    def own(axis, side, u):
        return KINDS["own", axis, side] * slots + u

    def copy_of(d):
        to = d if weight(d) == 1 else (d[0], 0, d[2])
        e = (-to[0], d[1] if weight(d) > 1 else -d[1], -to[2])
        if weight(d) > 1:
            src, dst = gone.at[OFFSETS.index(d)], came.at[OFFSETS.index(e)]
        else:
            axis = [i for i in range(3) if d[i]][0]
            into = entry_of(e) * slots
            dst = pool.at[into : into + slots]
            kept = own(axis, last(-d[axis]), 0)
            src = pool.at[kept : kept + slots]
        return pltpu.make_async_remote_copy(
            src_ref=src,
            dst_ref=dst,
            send_sem=send_sem.at[OFFSETS.index(d)],
            recv_sem=recv_sem.at[OFFSETS.index(e)],
            device_id=target(to),
            device_id_type=MESH,
        )

    def start(d):
        @pl.when(exists(d))
        def _():
            copy_of(d).start()

    def sender(e):
        return (-e[0], e[1] if weight(e) > 1 else -e[1], -e[2])

    for u in range(slots):
        pool[ZERO * slots + u] = jnp.zeros(pool.shape[1:], pool.dtype)
        for end in (0, 17):
            planes[u, end] = jnp.zeros(planes.shape[2:], planes.dtype)
    others[0].wait()
    depth = 3 * channels
    for a in range(3):
        for b in range(3):
            at = (a * 9 + b * 3) * channels
            taps = cw[:, at : at + depth]
            w[b * cout : (b + 1) * cout, a * depth : (a + 1) * depth] = taps
            if a != 1:
                wf[last(a - 1), b * cout : (b + 1) * cout, :] = taps
            if b != 1:
                wf[2 + last(b - 1), a * cout : (a + 1) * cout, :] = taps
            for k in (0, 2):
                wf[4 + k // 2, b * cout : (b + 1) * cout, a * channels : (a + 1) * channels] = taps[
                    :, k * channels : (k + 1) * channels
                ]

    for other in others[1:]:
        other.wait()
    value = jnp.dot(links[...].astype(F32), table[16 : 16 + links.shape[1], :].astype(F32), preferred_element_type=F32)
    value = value.astype(jnp.int32)
    code, slot = value >> 1, value & 1
    entry, lies = jnp.full_like(value, -1), jnp.zeros_like(value)
    for c in range(8):
        entry = jnp.where(code == c, table[c : c + 1, :], entry)
        lies = jnp.where(code == c, table[8 + c : 9 + c, :], lies)
    needed = jnp.dot(
        jnp.where(entry >= 0, 1.0, 0.0), table[48:176, :].astype(F32), preferred_element_type=F32
    ).astype(jnp.int32)
    meta[0:slots, :] = jnp.where(entry >= 0, entry + slot, ZERO * slots)
    meta[slots : 2 * slots, :] = lies
    meta[2 * slots : 3 * slots, :] = needed
    eye = lax.broadcasted_iota(jnp.int32, (cout, cout), 0) == lax.broadcasted_iota(jnp.int32, (cout, cout), 1)
    for i in (0, 1):
        column = jnp.sum(jnp.where(eye, biases[i : i + 1, :], 0.0), axis=1, keepdims=True)
        bias[i] = jnp.zeros(bias.shape[1:], F32) + column

    for load in loads:
        load.wait()

    lane = lax.broadcasted_iota(jnp.int32, (channels, 128), 1)
    group, place = lane // 16, lane % 16
    third = channels // 3
    cut = lax.broadcasted_iota(jnp.int32, (third, 128), 1)
    cut_group, cut_place = cut // 16, cut % 16

    def tile(u, x, half):
        at = x * 256 + half * 128
        return blk[u, :, at : at + 128]

    def third_of(entry, part, half):
        return pool[entry, part * third : part * third + third, half * 128 : half * 128 + 128]

    for u in range(slots):
        for half in (0, 1):
            before, after = None, None
            for k in range(8):
                x = half * 8 + k
                moved = roll(jnp.where(group == 7, tile(u, x, 1), tile(u, x, 0)), k * 16)
                after = moved if after is None else jnp.where(group == k, moved, after)
                before = moved if before is None else jnp.where(group == (k + 7) % 8, moved, before)
            lanes = slice(half * 128, half * 128 + 128)
            pool[own(1, 0, u), :, lanes] = roll(before, 16)
            pool[own(1, 1, u), :, lanes] = after
    pl.semaphore_wait(barrier, (1 + near["gx"]) * (1 + near["gz"]) - 1 + near["gy"] + extra)
    for slot in range(slots)[::-1]:
        for step in (1, -1):
            @pl.when(exists((step, 0, 0)))
            def _():
                direct, around = halves(step, slot)
                if slot < slots - 1:
                    direct.start()
                    return
                pl.when(turns(step))(around.start)
                pl.when(jnp.logical_not(turns(step)))(direct.start)
    start((0, 1, 0))
    start((0, -1, 0))
    for u in range(slots):
        for half in (0, 1):
            before, after = None, None
            for x in range(16):
                moved = roll(tile(u, x, half), x)
                after = moved if after is None else jnp.where(place == x, moved, after)
                before = moved if before is None else jnp.where(place == (x + 15) % 16, moved, before)
            lanes = slice(half * 128, half * 128 + 128)
            pool[own(2, 0, u), :, lanes] = roll(before, -15)
            pool[own(2, 1, u), :, lanes] = after
    start((0, 0, 1))
    start((0, 0, -1))
    for u in range(slots):
        pool[own(0, 0, u)] = blk[u, :, 15 * 256 : 16 * 256]
        pool[own(0, 1, u)] = blk[u, :, 0:256]

    def strips(d, entry, col):
        made = None
        for part in range(3):
            for u in range(slots):
                for half in (0, 1):
                    goes = (part * slots + u) * 2 + half
                    moved = roll(third_of(entry(u), part, half), goes - col)
                    made = moved if made is None else jnp.where(cut_place == goes, moved, made)
        return made

    def corner_lane(dy, u, part):
        return part * 16 + 12 + last(dy) * slots + u

    for dy in (-1, 1):
        @pl.when(exists((0, dy, 0)))
        def _():
            copy_of((0, -dy, 0)).wait_recv()
    for dy in (-1, 1):
        @pl.when(exists((0, dy, 0)))
        def _():
            def entry(u):
                return KINDS["came", 1, last(dy)] * slots + u

            for dx in (1, -1):
                made = None
                for part in range(3):
                    for u in range(slots):
                        goes = part * slots + u
                        half = 1 if dx == 1 else 0
                        moved = roll(third_of(entry(u), part, half), (goes - 7 * half) * 16)
                        made = moved if made is None else jnp.where(cut_group == goes, moved, made)
                gone[OFFSETS.index((dx, dy, 0))] = made
                start((dx, dy, 0))
            for dz in (1, -1):
                gone[OFFSETS.index((0, dy, dz))] = strips((0, dy, dz), entry, 15 if dz == 1 else 0)
                start((0, dy, dz))
    for dx in (1, -1):
        for dz in (1, -1):
            x, z = (15 if dx == 1 else 0), (15 if dz == 1 else 0)
            made = strips((dx, 0, dz), lambda u: own(2, last(-dz), u), x)
            for dy in (-1, 1):
                for u in range(slots):
                    for part in range(3):
                        goes = corner_lane(dy, u, part)
                        half = x // 8
                        moved = roll(
                            third_of(KINDS["came", 1, last(dy)] * slots + u, part, half), goes - (x * 16 + z) % 128
                        )
                        made = jnp.where(cut == goes, moved, made)
            gone[OFFSETS.index((dx, 0, dz))] = made
            start((dx, 0, dz))

    def build(u, p):
        for half in (0, 1):
            lanes = slice(128 * half, 128 * half + 128)
            value = blk[u, :, (p - 1) * 256 + 128 * half : (p - 1) * 256 + 128 * half + 128]
            planes[u, p, channels : 2 * channels, lanes] = value
            for dz in (-1, 1):
                moved = jnp.where(place == (0 if dz == -1 else 15), jnp.zeros_like(value), roll(value, -dz))
                planes[u, p, (dz + 1) * channels : (dz + 2) * channels, lanes] = moved

    def per_slot(u, _):
        build(u, 1)
        for x in range(16):
            if x < 15:
                build(u, x + 2)
            y = jnp.dot(w[...], planes[u, x : x + 3].reshape(3 * depth, 256), preferred_element_type=F32)
            acc[u, x, :, 0:128], acc[u, x, :, 128:256] = rows_of(y, cout)
        return 0

    per_slot(0, 0)
    for step in (1, -1):
        @pl.when(relays(here["gx"], step))
        def _():
            halves(step, slots - 1)[1].wait_recv()
            pass_on(step).start()

    for u in range(1, slots):
        per_slot(u, 0)

    for e in sorted(messages, key=lambda e: -weight(e)):
        @pl.when(exists(e))
        def _():
            if weight(e) == 1 and e[0]:
                for slot in range(slots):
                    halves(-e[0], slot)[0].wait_recv()
            elif weight(e) > 1 or not e[1]:
                copy_of(sender(e)).wait_recv()
            if weight(e) == 1:
                return
            got = came[OFFSETS.index(e)]
            for u in range(slots):
                for part in range(3):
                    rows = slice(part * third, part * third + third)
                    if not e[2]:
                        pool[KINDS[e] * slots + u, rows, 0:128] = roll(got, -16 * (part * slots + u))
                        continue
                    for half in (0, 1):
                        lies = (part * slots + u) * 2 + half
                        col = far(e[2] if e[1] else e[0])
                        pool[KINDS[e] * slots + u, rows, half * 128 : half * 128 + 128] = roll(got, col - lies)
                    if not e[1]:
                        for dy in (-1, 1):
                            pool[KINDS[e[0], dy, e[2]] * slots + u, rows, 0:128] = roll(got, -corner_lane(dy, u, part))
    for d in messages:
        @pl.when(exists(d))
        def _():
            if weight(d) > 1 or not d[0]:
                copy_of(d).wait_send()
            else:
                for slot in range(slots):
                    halves(d[0], slot)[0].wait_send()
    for step in (1, -1):
        pl.when(relays(here["gx"], step))(lambda: pass_on(step).wait_send())


def finish_kernel(slots, meta, count, acc, pool, wf, bias, hw, out, stack, ring, faces, made, out_sem):
    channels = pool.shape[1]
    cout = hw.shape[0]
    lane = lax.broadcasted_iota(jnp.int32, (channels, 128), 1)
    group, place = lane // 16, lane % 16
    lane_out = lax.broadcasted_iota(jnp.int32, (cout, 128), 1)
    group_out, place_out = lane_out // 16, lane_out % 16
    at_ends = jnp.logical_or(place_out == 0, place_out == 15)
    row_bias, head_bias = bias[0], bias[1]
    both_head = jnp.concatenate([head_bias, head_bias], 1)

    def entry(s, f, k):
        return meta[s, f * PARTS + k]

    def fetch(s, f, k, goes):
        lies = meta[slots + s, f * PARTS + k]
        got = pool[entry(s, f, k), :, pl.ds(pl.multiple_of((lies // 128) * 128, 128), 128)]
        return pltpu.roll(got, lax.rem(goes - lies + 256, 128), 1)

    def face(s, f):
        for half in (0, 1):
            lanes = slice(half * 128, half * 128 + 128)
            value = pool[entry(s, f, 0), :, lanes]
            stack[f, channels : 2 * channels, lanes] = value
            for e in (-1, 1):
                at = 0 if e == -1 else 15
                piece = roll(pool[entry(s, f, 1 + last(e)), :, lanes], 15 * e)
                stack[f, (e + 1) * channels : (e + 2) * channels, lanes] = jnp.where(
                    place == at, piece, roll(value, -e)
                )
        y = jnp.dot(wf[f], stack[f], preferred_element_type=F32)
        faces[f, :, 0:128], faces[f, :, 128:256] = rows_of(y, cout)

    def rings(s, axis):
        line = None
        for i in (0, 1):
            for r in (0, 1):
                goes = 1 - i if r else 6 + i
                got = fetch(s, 2 * axis + i, 3 + r, goes * 16)
                line = got if line is None else jnp.where(group == goes, got, line)
        ring[channels : 2 * channels, :] = line
        for e in (-1, 1):
            at = 0 if e == -1 else 15
            moved = jnp.where(place == at, jnp.zeros_like(line), roll(line, -e))
            if axis == 0:
                for i in (0, 1):
                    for r in (0, 1):
                        goes = (1 - i if r else 6 + i) * 16 + at
                        moved = jnp.where(lane == goes, fetch(s, i, 5 + 2 * last(e) + r, goes), moved)
            ring[(e + 1) * channels : (e + 2) * channels, :] = moved
        for i in (0, 1):
            f = 2 * axis + i
            y = jnp.dot(wf[f], ring[...], preferred_element_type=F32)
            faces[f, :, 0:128] += jnp.where(group_out == 0, roll(y[0:cout], 32 - 16 * i), 0.0)
            faces[f, :, 128:256] += jnp.where(group_out == 7, roll(y[2 * cout :], -32 + 16 * i), 0.0)

    def plane(s, x, keep, with_faces, with_y, with_z):
        hidden = []
        for half in (0, 1):
            lanes = slice(half * 128, half * 128 + 128)
            v = acc[s, x, :, lanes] + row_bias
            if with_faces and x in (0, 15):
                v = v + faces[x // 15, :, lanes]
            if with_y:
                goes = 7 if half else 0
                strip = faces[2 + half, :, (x // 8) * 128 : (x // 8) * 128 + 128]
                v = v + jnp.where(group_out == goes, roll(strip, (goes - x % 8) * 16), 0.0)
            if with_z:
                ends = jnp.where(place_out == x, faces[4, :, lanes], faces[5, :, lanes])
                v = v + jnp.where(at_ends, roll(ends, -x), 0.0)
            hidden.append(jnp.maximum(v, 0.0).astype(BF16))
        mixed = jnp.dot(hw[...], jnp.concatenate(hidden, 1), preferred_element_type=F32) + both_head
        made[s, :, x * 256 : x * 256 + 256] = (mixed * keep).astype(made.dtype)

    def chunk(s, q):
        lanes = pl.ds(q * 1024, 1024)
        return pltpu.make_async_copy(made.at[s, :, lanes], out.at[s, :, lanes], out_sem.at[s, q])

    def per_slot(s, _):
        keep = jnp.where(s < count[0, 0, 0], 1.0, 0.0)
        any_face = meta[2 * slots + s, FACE] > 0
        any_y = meta[2 * slots + s, SIDE_Y] > 0
        any_z = meta[2 * slots + s, SIDE_Z] > 0

        @pl.when(any_face)
        def _():
            for f in range(6):
                face(s, f)
            for axis in (0, 2):
                pl.when(meta[2 * slots + s, RING + axis] > 0)(functools.partial(rings, s, axis))

        def run(with_faces, with_y, with_z):
            if with_z:
                for half in (0, 1):
                    lanes = slice(half * 128, half * 128 + 128)
                    faces[5, :, lanes] = roll(faces[5, :, lanes], 15)
            for q in range(4):
                for k in range(4):
                    plane(s, q * 4 + k, keep, with_faces, with_y, with_z)
                chunk(s, q).start()

        for with_y in (True, False):
            for with_z in (True, False):
                chosen = jnp.logical_and(
                    any_y if with_y else jnp.logical_not(any_y), any_z if with_z else jnp.logical_not(any_z)
                )
                chosen = jnp.logical_and(any_face, chosen)
                pl.when(chosen)(functools.partial(run, True, with_y, with_z))
        pl.when(jnp.logical_not(any_face))(functools.partial(run, False, False, False))
        return 0

    lax.fori_loop(0, slots, per_slot, 0)
    for s in range(slots):
        for q in range(4):
            chunk(s, q).wait()


def finish(slots, voxels, meta, block_count, acc, pool, wf, bias, head_weight):
    channels = pool.shape[1]
    cout = head_weight.shape[0]
    return pl.pallas_call(
        functools.partial(finish_kernel, slots),
        out_shape=jax.ShapeDtypeStruct((slots, cout, voxels), BF16),
        in_specs=[pl.BlockSpec(memory_space=pltpu.SMEM)] * 2 + [pl.BlockSpec(memory_space=pltpu.VMEM)] * 5,
        out_specs=pl.BlockSpec(memory_space=pltpu.HBM),
        scratch_shapes=[
            pltpu.VMEM((6, 3 * channels, 256), BF16),
            pltpu.VMEM((3 * channels, 128), BF16),
            pltpu.VMEM((6, cout, 256), F32),
            pltpu.VMEM((slots, cout, voxels), BF16),
            pltpu.SemaphoreType.DMA((slots, 4)),
        ],
        compiler_params=pltpu.CompilerParams(vmem_limit_bytes=20 << 20),
        name="finish",
    )(meta, block_count, acc, pool, wf, bias, head_weight)


def body(sizes, row, blocks, block_count, neighbours, conv_weight, conv_bias, head_weight, head_bias):
    slots, channels, voxels = blocks.shape[2:]
    cout = head_weight.shape[0]
    vmem = pl.BlockSpec(memory_space=pltpu.VMEM)
    hbm = pl.BlockSpec(memory_space=pltpu.HBM)
    table = jnp.asarray(plan(slots))
    operands = [blocks.reshape(slots, channels, voxels), conv_weight, neighbours.reshape(slots, 26), table, conv_bias[None], head_bias[None]]
    acc, pool, wf, meta, bias = pl.pallas_call(
        functools.partial(exchange_kernel, sizes, row, slots),
        out_shape=[
            jax.ShapeDtypeStruct((slots, 16, cout, 256), F32),
            jax.ShapeDtypeStruct(((ZERO + 1) * slots, channels, 256), blocks.dtype),
            jax.ShapeDtypeStruct((6, 3 * cout, 3 * channels), BF16),
            jax.ShapeDtypeStruct((4 * slots, 128), jnp.int32),
            jax.ShapeDtypeStruct((2, cout, 128), F32),
        ],
        in_specs=[hbm] * 6,
        out_specs=[vmem] * 5,
        scratch_shapes=[
            pltpu.VMEM((slots, channels, voxels), BF16),
            pltpu.VMEM((slots, 18, 3 * channels, 256), BF16),
            pltpu.VMEM((3 * cout, 9 * channels), BF16),
            pltpu.VMEM(conv_weight.shape, BF16),
            pltpu.VMEM((slots, 26), jnp.int32),
            pltpu.VMEM(table.shape, jnp.int32),
            pltpu.VMEM((2, cout), F32),
            pltpu.VMEM((27, channels // 3, 128), BF16),
            pltpu.VMEM((27, channels // 3, 128), BF16),
            pltpu.VMEM((2, channels, 256), BF16),
            pltpu.SemaphoreType.DMA((slots, 2)),
            pltpu.SemaphoreType.DMA((5,)),
            pltpu.SemaphoreType.DMA((27,)),
            pltpu.SemaphoreType.DMA((27,)),
            pltpu.SemaphoreType.DMA((2, slots)),
            pltpu.SemaphoreType.DMA((2, slots)),
            pltpu.SemaphoreType.DMA((2,)),
            pltpu.SemaphoreType.DMA((2,)),
        ],
        compiler_params=pltpu.CompilerParams(collective_id=0, has_side_effects=True, vmem_limit_bytes=24 << 20),
        name="exchange",
    )(*[pltpu.with_memory_space_constraint(operand, pltpu.HBM) for operand in operands])
    out = finish(slots, voxels, meta, block_count, acc, pool, wf, bias, head_weight)
    return out.reshape(1, 1, slots, cout, voxels)


def row_length(mesh):
    axis = mesh.axis_names.index("gx")
    line = np.moveaxis(mesh.devices, axis, 0).reshape(mesh.shape["gx"], -1)[:, 0]
    coords = [np.asarray(device.coords) for device in line]
    for i in range(1, len(coords)):
        if np.count_nonzero(coords[i] != coords[i - 1]) > 1:
            return i
    return 0


def solution(mesh):
    placed = (
        P("gx", "gz", "gy", None, None),
        P("gx", "gz", "gy"),
        P("gx", "gz", "gy", None),
        P(),
        P(),
        P(),
        P(),
    )
    return jax.shard_map(
        functools.partial(body, dict(mesh.shape), row_length(mesh)),
        mesh=mesh,
        in_specs=placed,
        out_specs=P("gx", "gz", "gy", None, None),
        check_vma=False,
    )
```

```python
import functools

import jax
import jax.numpy as jnp
import numpy as np
from jax import lax
from jax.experimental import pallas as pl
from jax.experimental.pallas import tpu as pltpu
from jax.sharding import PartitionSpec as P

AXES = ("gx", "gy", "gz")
OFFSETS = [(a, b, c) for a in (-1, 0, 1) for b in (-1, 0, 1) for c in (-1, 0, 1)]
LINKS = [o for o in OFFSETS if o != (0, 0, 0)]
F32 = jnp.float32
BF16 = jnp.bfloat16
MESH = pl.DeviceIdType.MESH


def weight(d):
    return sum(map(abs, d))


def last(step):
    return 0 if step == -1 else 1


def far(step):
    return 15 if step == -1 else 0


KINDS = {("own", a, s): 2 * a + s for a in range(3) for s in (0, 1)}
KINDS |= {("came", a, s): 6 + 2 * a + s for a in range(3) for s in (0, 1)}
for _d in LINKS:
    if weight(_d) > 1:
        KINDS[_d] = len(KINDS)
ZERO = len(KINDS)


def entry_of(d):
    if weight(d) > 1:
        return KINDS[d]
    axis = [i for i in range(3) if d[i]][0]
    return KINDS["came", axis, last(d[axis])]


def piece_of(o, c):
    e = tuple(o[a] if c >> a & 1 else 0 for a in range(3))
    if c:
        kind = entry_of(e)
    else:
        axis = [a for a in range(3) if o[a]][0]
        kind = KINDS["own", axis, last(o[axis])]
    x, y, z = (far(step) if step else 0 for step in o)
    if c == 7:
        lane = 0
    elif c == 3:
        lane = z
    elif c in (4, 5):
        lane = y * 16 + x
    elif c in (2, 6) or not o[0]:
        lane = x * 16 + z
    else:
        lane = y * 16 + z
    return kind, lane


PARTS = 9
FACE, RING = 0, 3


def face_parts(axis, step):
    def off(**steps):
        return tuple(steps.get(name, 0) for name in "xyz")

    name = "xyz"[axis]
    parts = [(off(**{name: step}), {0: (0, 1), 1: (0, 2), 2: (0, 4)}[axis])]
    for e in (-1, 1):
        parts.append((off(**{name: step, "x" if axis == 2 else "z": e}), {0: (0, 1), 1: (0, 2, 6), 2: (4, 5)}[axis]))
    for r in (-1, 1):
        if axis == 1:
            parts.append((off(y=step), ()))
        else:
            parts.append((off(**{name: step, "y": r}), {0: (0, 1, 2, 3), 2: (4,)}[axis]))
    for e in (-1, 1):
        for r in (-1, 1):
            parts.append((off(x=step, y=r, z=e), tuple(range(8))) if axis == 0 else (off(**{name: step}), ()))
    return parts


def plan(slots):
    entry = np.full((8, 128), -1, np.int32)
    lane = np.zeros((8, 128), np.int32)
    pick = np.zeros((32, 128), np.int32)
    needs = np.zeros((128, 128), np.int32)
    for f in range(6):
        for k, (o, codes) in enumerate(face_parts(f // 2, (-1, 1)[f % 2])):
            j = f * PARTS + k
            pick[LINKS.index(o), j] = 1
            for c in codes:
                if any(c >> a & 1 and o[a] == 0 for a in range(3)):
                    continue
                kind, at = piece_of(o, c)
                entry[c, j], lane[c, j] = kind * slots, at
            needs[j, FACE + f // 2] = 1
            needs[j, RING + f // 2] = k >= 3
    return np.concatenate([entry, lane, pick, needs])


def roll(value, shift):
    shift %= 128
    return pltpu.roll(value, shift, 1) if shift else value


def rows_of(y, cout):
    lane = lax.broadcasted_iota(jnp.int32, (cout, 128), 1)
    first, final = lane < 16, lane >= 112
    down = [roll(y[0:cout, at : at + 128], 16) for at in (0, 128)]
    up = [roll(y[2 * cout :, at : at + 128], -16) for at in (0, 128)]
    zero = jnp.zeros_like(down[0])
    low = y[cout : 2 * cout, 0:128] + jnp.where(first, zero, down[0]) + jnp.where(final, up[1], up[0])
    high = y[cout : 2 * cout, 128:256] + jnp.where(first, down[0], down[1]) + jnp.where(final, zero, up[1])
    return low, high


def exchange_kernel(
    sizes, row, slots, blk_hbm, cw_hbm, links_hbm, plan_hbm, cb_hbm, hb_hbm, acc, pool, wf, meta, bias,
    blk, planes, w, cw, links, table, biases, gone, came, passed, load_sem, aux_sem, send_sem, recv_sem, half_send, half_recv, pass_send, pass_recv,
):
    channels = blk.shape[1]
    cout = w.shape[0] // 3
    here = {axis: lax.axis_index(axis) for axis in AXES}

    def exists(d):
        ok = None
        for axis, step in zip(AXES, d):
            if step:
                at = here[axis] + step
                good = jnp.logical_and(at >= 0, at < sizes[axis])
                ok = good if ok is None else jnp.logical_and(ok, good)
        return ok

    def target(d):
        return {axis: here[axis] + step for axis, step in zip(AXES, d) if step}

    def turn(at, step):
        if not row:
            return at < 0
        inside = jnp.logical_and(at + step >= 0, at + step < sizes["gx"])
        return jnp.logical_and(inside, lax.rem(at + row, row) == (row - 1 if step == 1 else 0))

    def via(at, step):
        return at + step * (row)

    def relays(at, step):
        origin = at - step * (row)
        known = jnp.logical_and(origin >= 0, origin < sizes["gx"])
        return jnp.logical_and(known, turn(origin, step))

    def halves(step, slot):
        x = 15 if step == 1 else 0
        side = last(-step)
        src = blk_hbm.at[slot, :, x * 256 : x * 256 + 256]
        into = KINDS["came", 0, side] * slots + slot
        sems = dict(send_sem=half_send.at[side, slot], device_id_type=MESH)
        direct = pltpu.make_async_remote_copy(
            src_ref=src, dst_ref=pool.at[into], recv_sem=half_recv.at[side, slot],
            device_id={"gx": here["gx"] + step}, **sems,
        )
        around = pltpu.make_async_remote_copy(
            src_ref=src, dst_ref=passed.at[side], recv_sem=pass_recv.at[side],
            device_id={"gx": via(here["gx"], step)}, **sems,
        )
        return direct, around

    def pass_on(step):
        side = last(-step)
        into = KINDS["came", 0, side] * slots + slots - 1
        return pltpu.make_async_remote_copy(
            src_ref=passed.at[side], dst_ref=pool.at[into], send_sem=pass_send.at[side],
            recv_sem=half_recv.at[side, slots - 1],
            device_id={"gx": here["gx"] - step * ((row) - 1)}, device_id_type=MESH,
        )

    def turns(step):
        return turn(here["gx"], step)

    partners = [d for d in LINKS if not d[1] or weight(d) == 1]
    messages = [d for d in LINKS if weight(d) < 3]
    span = blk.shape[2] // 2
    loads = [
        pltpu.make_async_copy(
            blk_hbm.at[u, :, k * span : k * span + span], blk.at[u, :, k * span : k * span + span], load_sem.at[u, k]
        )
        for u in range(slots)
        for k in (0, 1)
    ]
    others = [
        pltpu.make_async_copy(src, dst, aux_sem.at[i])
        for i, (src, dst) in enumerate([(cw_hbm, cw), (links_hbm, links), (plan_hbm, table), (cb_hbm, biases.at[0:1]), (hb_hbm, biases.at[1:2])])
    ]
    for other in others:
        other.start()
    for load in loads:
        load.start()
    barrier = pltpu.get_barrier_semaphore()
    for d in partners:
        @pl.when(exists(d))
        def _():
            pl.semaphore_signal(barrier, inc=1, device_id=target(d), device_id_type=MESH)
    def greet(when, device):
        @pl.when(when)
        def _():
            pl.semaphore_signal(barrier, inc=1, device_id={"gx": device}, device_id_type=MESH)

    extra = 0
    for step in (-1, 1):
        origin = here["gx"] - step * (row)
        greet(relays(here["gx"], step), origin)
        extra = extra + jnp.where(turns(step), 1, 0)
        if row > 2:
            greet(turn(here["gx"] - step, step), via(here["gx"] - step, step))
            extra = extra + jnp.where(relays(here["gx"], step), 1, 0)
    near = {
        axis: jnp.where(here[axis] > 0, 1, 0) + jnp.where(here[axis] < sizes[axis] - 1, 1, 0) for axis in AXES
    }

    def own(axis, side, u):
        return KINDS["own", axis, side] * slots + u

    def copy_of(d):
        to = d if weight(d) == 1 else (d[0], 0, d[2])
        e = (-to[0], d[1] if weight(d) > 1 else -d[1], -to[2])
        if weight(d) > 1:
            src, dst = gone.at[OFFSETS.index(d)], came.at[OFFSETS.index(e)]
        else:
            axis = [i for i in range(3) if d[i]][0]
            into = entry_of(e) * slots
            dst = pool.at[into : into + slots]
            kept = own(axis, last(-d[axis]), 0)
            src = pool.at[kept : kept + slots]
        return pltpu.make_async_remote_copy(
            src_ref=src,
            dst_ref=dst,
            send_sem=send_sem.at[OFFSETS.index(d)],
            recv_sem=recv_sem.at[OFFSETS.index(e)],
            device_id=target(to),
            device_id_type=MESH,
        )

    def start(d):
        @pl.when(exists(d))
        def _():
            copy_of(d).start()

    def sender(e):
        return (-e[0], e[1] if weight(e) > 1 else -e[1], -e[2])

    for u in range(slots):
        pool[ZERO * slots + u] = jnp.zeros(pool.shape[1:], pool.dtype)
        for end in (0, 17):
            planes[u, end] = jnp.zeros(planes.shape[2:], planes.dtype)
    others[0].wait()
    depth = 3 * channels
    for a in range(3):
        for b in range(3):
            at = (a * 9 + b * 3) * channels
            taps = cw[:, at : at + depth]
            w[b * cout : (b + 1) * cout, a * depth : (a + 1) * depth] = taps
            if a != 1:
                wf[last(a - 1), b * cout : (b + 1) * cout, :] = taps
            if b != 1:
                wf[2 + last(b - 1), a * cout : (a + 1) * cout, :] = taps
            for k in (0, 2):
                wf[4 + k // 2, b * cout : (b + 1) * cout, a * channels : (a + 1) * channels] = taps[
                    :, k * channels : (k + 1) * channels
                ]

    for other in others[1:]:
        other.wait()
    value = jnp.dot(links[...].astype(F32), table[16 : 16 + links.shape[1], :].astype(F32), preferred_element_type=F32)
    value = value.astype(jnp.int32)
    code, slot = value >> 1, value & 1
    entry, lies = jnp.full_like(value, -1), jnp.zeros_like(value)
    for c in range(8):
        entry = jnp.where(code == c, table[c : c + 1, :], entry)
        lies = jnp.where(code == c, table[8 + c : 9 + c, :], lies)
    needed = jnp.dot(
        jnp.where(entry >= 0, 1.0, 0.0), table[48:176, :].astype(F32), preferred_element_type=F32
    ).astype(jnp.int32)
    meta[0:slots, :] = jnp.where(entry >= 0, entry + slot, ZERO * slots)
    meta[slots : 2 * slots, :] = lies
    meta[2 * slots : 3 * slots, :] = needed
    eye = lax.broadcasted_iota(jnp.int32, (cout, cout), 0) == lax.broadcasted_iota(jnp.int32, (cout, cout), 1)
    for i in (0, 1):
        column = jnp.sum(jnp.where(eye, biases[i : i + 1, :], 0.0), axis=1, keepdims=True)
        bias[i] = jnp.zeros(bias.shape[1:], F32) + column

    for load in loads:
        load.wait()

    lane = lax.broadcasted_iota(jnp.int32, (channels, 128), 1)
    group, place = lane // 16, lane % 16
    third = channels // 3
    cut = lax.broadcasted_iota(jnp.int32, (third, 128), 1)
    cut_group, cut_place = cut // 16, cut % 16

    def tile(u, x, half):
        at = x * 256 + half * 128
        return blk[u, :, at : at + 128]

    def third_of(entry, part, half):
        return pool[entry, part * third : part * third + third, half * 128 : half * 128 + 128]

    for u in range(slots):
        for half in (0, 1):
            before, after = None, None
            for k in range(8):
                x = half * 8 + k
                moved = roll(jnp.where(group == 7, tile(u, x, 1), tile(u, x, 0)), k * 16)
                after = moved if after is None else jnp.where(group == k, moved, after)
                before = moved if before is None else jnp.where(group == (k + 7) % 8, moved, before)
            lanes = slice(half * 128, half * 128 + 128)
            pool[own(1, 0, u), :, lanes] = roll(before, 16)
            pool[own(1, 1, u), :, lanes] = after
    pl.semaphore_wait(barrier, (1 + near["gx"]) * (1 + near["gz"]) - 1 + near["gy"] + extra)
    for slot in range(slots)[::-1]:
        for step in (1, -1):
            @pl.when(exists((step, 0, 0)))
            def _():
                direct, around = halves(step, slot)
                if slot < slots - 1:
                    direct.start()
                    return
                pl.when(turns(step))(around.start)
                pl.when(jnp.logical_not(turns(step)))(direct.start)
    start((0, 1, 0))
    start((0, -1, 0))
    for u in range(slots):
        for half in (0, 1):
            before, after = None, None
            for x in range(16):
                moved = roll(tile(u, x, half), x)
                after = moved if after is None else jnp.where(place == x, moved, after)
                before = moved if before is None else jnp.where(place == (x + 15) % 16, moved, before)
            lanes = slice(half * 128, half * 128 + 128)
            pool[own(2, 0, u), :, lanes] = roll(before, -15)
            pool[own(2, 1, u), :, lanes] = after
    start((0, 0, 1))
    start((0, 0, -1))
    for u in range(slots):
        pool[own(0, 0, u)] = blk[u, :, 15 * 256 : 16 * 256]
        pool[own(0, 1, u)] = blk[u, :, 0:256]

    def strips(d, entry, col):
        made = None
        for part in range(3):
            for u in range(slots):
                for half in (0, 1):
                    goes = (part * slots + u) * 2 + half
                    moved = roll(third_of(entry(u), part, half), goes - col)
                    made = moved if made is None else jnp.where(cut_place == goes, moved, made)
        return made

    def corner_lane(dy, u, part):
        return part * 16 + 12 + last(dy) * slots + u

    for dy in (-1, 1):
        @pl.when(exists((0, dy, 0)))
        def _():
            copy_of((0, -dy, 0)).wait_recv()
    for dy in (-1, 1):
        @pl.when(exists((0, dy, 0)))
        def _():
            def entry(u):
                return KINDS["came", 1, last(dy)] * slots + u

            for dx in (1, -1):
                made = None
                for part in range(3):
                    for u in range(slots):
                        goes = part * slots + u
                        half = 1 if dx == 1 else 0
                        moved = roll(third_of(entry(u), part, half), (goes - 7 * half) * 16)
                        made = moved if made is None else jnp.where(cut_group == goes, moved, made)
                gone[OFFSETS.index((dx, dy, 0))] = made
                start((dx, dy, 0))
            for dz in (1, -1):
                gone[OFFSETS.index((0, dy, dz))] = strips((0, dy, dz), entry, 15 if dz == 1 else 0)
                start((0, dy, dz))
    for dx in (1, -1):
        for dz in (1, -1):
            x, z = (15 if dx == 1 else 0), (15 if dz == 1 else 0)
            made = strips((dx, 0, dz), lambda u: own(2, last(-dz), u), x)
            for dy in (-1, 1):
                for u in range(slots):
                    for part in range(3):
                        goes = corner_lane(dy, u, part)
                        half = x // 8
                        moved = roll(
                            third_of(KINDS["came", 1, last(dy)] * slots + u, part, half), goes - (x * 16 + z) % 128
                        )
                        made = jnp.where(cut == goes, moved, made)
            gone[OFFSETS.index((dx, 0, dz))] = made
            start((dx, 0, dz))

    def build(u, p):
        for half in (0, 1):
            lanes = slice(128 * half, 128 * half + 128)
            value = blk[u, :, (p - 1) * 256 + 128 * half : (p - 1) * 256 + 128 * half + 128]
            planes[u, p, channels : 2 * channels, lanes] = value
            for dz in (-1, 1):
                moved = jnp.where(place == (0 if dz == -1 else 15), jnp.zeros_like(value), roll(value, -dz))
                planes[u, p, (dz + 1) * channels : (dz + 2) * channels, lanes] = moved

    def per_slot(u, _):
        build(u, 1)
        for x in range(16):
            if x < 15:
                build(u, x + 2)
            y = jnp.dot(w[...], planes[u, x : x + 3].reshape(3 * depth, 256), preferred_element_type=F32)
            acc[u, x, :, 0:128], acc[u, x, :, 128:256] = rows_of(y, cout)
        return 0

    per_slot(0, 0)
    for step in (1, -1):
        @pl.when(relays(here["gx"], step))
        def _():
            halves(step, slots - 1)[1].wait_recv()
            pass_on(step).start()

    for u in range(1, slots):
        per_slot(u, 0)

    for e in sorted(messages, key=lambda e: -weight(e)):
        @pl.when(exists(e))
        def _():
            if weight(e) == 1 and e[0]:
                for slot in range(slots):
                    halves(-e[0], slot)[0].wait_recv()
            elif weight(e) > 1 or not e[1]:
                copy_of(sender(e)).wait_recv()
            if weight(e) == 1:
                return
            got = came[OFFSETS.index(e)]
            for u in range(slots):
                for part in range(3):
                    rows = slice(part * third, part * third + third)
                    if not e[2]:
                        pool[KINDS[e] * slots + u, rows, 0:128] = roll(got, -16 * (part * slots + u))
                        continue
                    for half in (0, 1):
                        lies = (part * slots + u) * 2 + half
                        col = far(e[2] if e[1] else e[0])
                        pool[KINDS[e] * slots + u, rows, half * 128 : half * 128 + 128] = roll(got, col - lies)
                    if not e[1]:
                        for dy in (-1, 1):
                            pool[KINDS[e[0], dy, e[2]] * slots + u, rows, 0:128] = roll(got, -corner_lane(dy, u, part))
    for d in messages:
        @pl.when(exists(d))
        def _():
            if weight(d) > 1 or not d[0]:
                copy_of(d).wait_send()
            else:
                for slot in range(slots):
                    halves(d[0], slot)[0].wait_send()
    for step in (1, -1):
        pl.when(relays(here["gx"], step))(lambda: pass_on(step).wait_send())


def finish_kernel(slots, meta, count, acc, pool, wf, bias, hw, out, stack, ring, faces, made, out_sem):
    channels = pool.shape[1]
    cout = hw.shape[0]
    lane = lax.broadcasted_iota(jnp.int32, (channels, 128), 1)
    group, place = lane // 16, lane % 16
    lane_out = lax.broadcasted_iota(jnp.int32, (cout, 128), 1)
    group_out, place_out = lane_out // 16, lane_out % 16
    at_ends = jnp.logical_or(place_out == 0, place_out == 15)
    row_bias, head_bias = bias[0], bias[1]
    both_head = jnp.concatenate([head_bias, head_bias], 1)

    def entry(s, f, k):
        return meta[s, f * PARTS + k]

    def fetch(s, f, k, goes):
        lies = meta[slots + s, f * PARTS + k]
        got = pool[entry(s, f, k), :, pl.ds(pl.multiple_of((lies // 128) * 128, 128), 128)]
        return pltpu.roll(got, lax.rem(goes - lies + 256, 128), 1)

    def face(s, f):
        for half in (0, 1):
            lanes = slice(half * 128, half * 128 + 128)
            value = pool[entry(s, f, 0), :, lanes]
            stack[f, channels : 2 * channels, lanes] = value
            for e in (-1, 1):
                at = 0 if e == -1 else 15
                piece = roll(pool[entry(s, f, 1 + last(e)), :, lanes], 15 * e)
                stack[f, (e + 1) * channels : (e + 2) * channels, lanes] = jnp.where(
                    place == at, piece, roll(value, -e)
                )
        y = jnp.dot(wf[f], stack[f], preferred_element_type=F32)
        faces[f, :, 0:128], faces[f, :, 128:256] = rows_of(y, cout)

    def rings(s, axis):
        line = None
        for i in (0, 1):
            for r in (0, 1):
                goes = 1 - i if r else 6 + i
                got = fetch(s, 2 * axis + i, 3 + r, goes * 16)
                line = got if line is None else jnp.where(group == goes, got, line)
        ring[channels : 2 * channels, :] = line
        for e in (-1, 1):
            at = 0 if e == -1 else 15
            moved = jnp.where(place == at, jnp.zeros_like(line), roll(line, -e))
            if axis == 0:
                for i in (0, 1):
                    for r in (0, 1):
                        goes = (1 - i if r else 6 + i) * 16 + at
                        moved = jnp.where(lane == goes, fetch(s, i, 5 + 2 * last(e) + r, goes), moved)
            ring[(e + 1) * channels : (e + 2) * channels, :] = moved
        for i in (0, 1):
            f = 2 * axis + i
            y = jnp.dot(wf[f], ring[...], preferred_element_type=F32)
            faces[f, :, 0:128] += jnp.where(group_out == 0, roll(y[0:cout], 32 - 16 * i), 0.0)
            faces[f, :, 128:256] += jnp.where(group_out == 7, roll(y[2 * cout :], -32 + 16 * i), 0.0)

    def plane(s, x, keep, with_faces, with_y, with_z):
        hidden = []
        for half in (0, 1):
            lanes = slice(half * 128, half * 128 + 128)
            v = acc[s, x, :, lanes] + row_bias
            if with_faces and x in (0, 15):
                v = v + faces[x // 15, :, lanes]
            if with_y:
                goes = 7 if half else 0
                strip = faces[2 + half, :, (x // 8) * 128 : (x // 8) * 128 + 128]
                v = v + jnp.where(group_out == goes, roll(strip, (goes - x % 8) * 16), 0.0)
            if with_z:
                ends = jnp.where(place_out == x, faces[4, :, lanes], faces[5, :, lanes])
                v = v + jnp.where(at_ends, roll(ends, -x), 0.0)
            hidden.append(jnp.maximum(v, 0.0).astype(BF16))
        mixed = jnp.dot(hw[...], jnp.concatenate(hidden, 1), preferred_element_type=F32) + both_head
        made[s, :, x * 256 : x * 256 + 256] = (mixed * keep).astype(made.dtype)

    def chunk(s, q):
        lanes = pl.ds(q * 1024, 1024)
        return pltpu.make_async_copy(made.at[s, :, lanes], out.at[s, :, lanes], out_sem.at[s, q])

    def per_slot(s, _):
        keep = jnp.where(s < count[0, 0, 0], 1.0, 0.0)
        active = [meta[2 * slots + s, FACE + axis] > 0 for axis in range(3)]

        def by_faces(leaf, axes=(), axis=0):
            if axis == 3:
                leaf(axes)
                return
            pl.when(active[axis])(lambda: by_faces(leaf, axes + (axis,), axis + 1))
            pl.when(jnp.logical_not(active[axis]))(lambda: by_faces(leaf, axes, axis + 1))

        def compute(axes):
            for axis in axes:
                face(s, 2 * axis)
                face(s, 2 * axis + 1)

        by_faces(compute)
        for axis in (0, 2):
            pl.when(meta[2 * slots + s, RING + axis] > 0)(functools.partial(rings, s, axis))

        def run(with_faces, with_y, with_z):
            if with_z:
                for half in (0, 1):
                    lanes = slice(half * 128, half * 128 + 128)
                    faces[5, :, lanes] = roll(faces[5, :, lanes], 15)
            for q in range(4):
                for k in range(4):
                    plane(s, q * 4 + k, keep, with_faces, with_y, with_z)
                chunk(s, q).start()

        by_faces(lambda axes: run(*(axis in axes for axis in range(3))))
        return 0

    lax.fori_loop(0, slots, per_slot, 0)
    for s in range(slots):
        for q in range(4):
            chunk(s, q).wait()


def finish(slots, voxels, meta, block_count, acc, pool, wf, bias, head_weight):
    channels = pool.shape[1]
    cout = head_weight.shape[0]
    return pl.pallas_call(
        functools.partial(finish_kernel, slots),
        out_shape=jax.ShapeDtypeStruct((slots, cout, voxels), BF16),
        in_specs=[pl.BlockSpec(memory_space=pltpu.SMEM)] * 2 + [pl.BlockSpec(memory_space=pltpu.VMEM)] * 5,
        out_specs=pl.BlockSpec(memory_space=pltpu.HBM),
        scratch_shapes=[
            pltpu.VMEM((6, 3 * channels, 256), BF16),
            pltpu.VMEM((3 * channels, 128), BF16),
            pltpu.VMEM((6, cout, 256), F32),
            pltpu.VMEM((slots, cout, voxels), BF16),
            pltpu.SemaphoreType.DMA((slots, 4)),
        ],
        compiler_params=pltpu.CompilerParams(vmem_limit_bytes=20 << 20),
        name="finish",
    )(meta, block_count, acc, pool, wf, bias, head_weight)


def body(sizes, row, blocks, block_count, neighbours, conv_weight, conv_bias, head_weight, head_bias):
    slots, channels, voxels = blocks.shape[2:]
    cout = head_weight.shape[0]
    vmem = pl.BlockSpec(memory_space=pltpu.VMEM)
    hbm = pl.BlockSpec(memory_space=pltpu.HBM)
    table = jnp.asarray(plan(slots))
    operands = [blocks.reshape(slots, channels, voxels), conv_weight, neighbours.reshape(slots, 26), table, conv_bias[None], head_bias[None]]
    acc, pool, wf, meta, bias = pl.pallas_call(
        functools.partial(exchange_kernel, sizes, row, slots),
        out_shape=[
            jax.ShapeDtypeStruct((slots, 16, cout, 256), F32),
            jax.ShapeDtypeStruct(((ZERO + 1) * slots, channels, 256), blocks.dtype),
            jax.ShapeDtypeStruct((6, 3 * cout, 3 * channels), BF16),
            jax.ShapeDtypeStruct((4 * slots, 128), jnp.int32),
            jax.ShapeDtypeStruct((2, cout, 128), F32),
        ],
        in_specs=[hbm] * 6,
        out_specs=[vmem] * 5,
        scratch_shapes=[
            pltpu.VMEM((slots, channels, voxels), BF16),
            pltpu.VMEM((slots, 18, 3 * channels, 256), BF16),
            pltpu.VMEM((3 * cout, 9 * channels), BF16),
            pltpu.VMEM(conv_weight.shape, BF16),
            pltpu.VMEM((slots, 26), jnp.int32),
            pltpu.VMEM(table.shape, jnp.int32),
            pltpu.VMEM((2, cout), F32),
            pltpu.VMEM((27, channels // 3, 128), BF16),
            pltpu.VMEM((27, channels // 3, 128), BF16),
            pltpu.VMEM((2, channels, 256), BF16),
            pltpu.SemaphoreType.DMA((slots, 2)),
            pltpu.SemaphoreType.DMA((5,)),
            pltpu.SemaphoreType.DMA((27,)),
            pltpu.SemaphoreType.DMA((27,)),
            pltpu.SemaphoreType.DMA((2, slots)),
            pltpu.SemaphoreType.DMA((2, slots)),
            pltpu.SemaphoreType.DMA((2,)),
            pltpu.SemaphoreType.DMA((2,)),
        ],
        compiler_params=pltpu.CompilerParams(collective_id=0, has_side_effects=True, vmem_limit_bytes=24 << 20),
        name="exchange",
    )(*[pltpu.with_memory_space_constraint(operand, pltpu.HBM) for operand in operands])
    out = finish(slots, voxels, meta, block_count, acc, pool, wf, bias, head_weight)
    return out.reshape(1, 1, slots, cout, voxels)


def row_length(mesh):
    axis = mesh.axis_names.index("gx")
    line = np.moveaxis(mesh.devices, axis, 0).reshape(mesh.shape["gx"], -1)[:, 0]
    coords = [np.asarray(device.coords) for device in line]
    for i in range(1, len(coords)):
        if np.count_nonzero(coords[i] != coords[i - 1]) > 1:
            return i
    return 0


def solution(mesh):
    placed = (
        P("gx", "gz", "gy", None, None),
        P("gx", "gz", "gy"),
        P("gx", "gz", "gy", None),
        P(),
        P(),
        P(),
        P(),
    )
    return jax.shard_map(
        functools.partial(body, dict(mesh.shape), row_length(mesh)),
        mesh=mesh,
        in_specs=placed,
        out_specs=P("gx", "gz", "gy", None, None),
        check_vma=False,
    )
```
